32 devices in a mesh: dp: 4 (over z), expert: 8 (over y, x, core).
Axes of the slice: x: 2, y: 2, z: 4, core: 2. Of those that a mesh axis runs over, the one named last changes fastest.
Arguments:
- layer_input: bfloat16 [4096, 3584], P(('dp', 'expert')), may hold values from -6 to 6
- output_grad: bfloat16 [4096, 3584], P(('dp', 'expert')), may hold values from -2 to 2
- expert_ids: int32 [4096, 8], P(('dp', 'expert')), may hold values from 0 to 255, all different within a row
- gate_probs: bfloat16 [4096, 8], P(('dp', 'expert')), may hold values from 0.049804688 to 1
- placement: int32 [8], replicated, may hold values from 0 to 255, as said below
- gate_weight: bfloat16 [8, 3584, 1024], P('expert', None, 'dp'), as said below
- up_weight: bfloat16 [8, 3584, 1024], P('expert', None, 'dp'), as said below
- down_weight: bfloat16 [8, 1024, 3584], P('expert', 'dp'), as said below
Outputs:
- grad_tokens: bfloat16 [4096, 3584], P(('dp', 'expert'))
- grad_route: bfloat16 [4096, 8], P(('dp', 'expert'))
- grad_gate: bfloat16 [8, 3584, 1024], P('expert', None, 'dp')
- grad_up: bfloat16 [8, 3584, 1024], P('expert', None, 'dp')
- grad_down: bfloat16 [8, 1024, 3584], P('expert', 'dp')
The draws below stay inside these ranges and needn't reach their ends.
Inputs may be any that keep to these rules, and one draw needn't show every extreme that they name: `placement`: no expert stands on more than two slots; exactly 1 expert stand on two. `gate_weight`: slots that hold the same expert hold equal weights. `up_weight`: slots that hold the same expert hold equal weights. `down_weight`: slots that hold the same expert hold equal weights.
All inputs are finite; a program needn't handle non-finite values.
Results may differ from the reference program's by a relative error of at most 0.012.
Values may be sent and summed in bfloat16 or wider, within the bound.
A program may use at most 128 MiB of HBM per device.

```python
import math
import jax
import jax.numpy as jnp
from jax import lax

D = 3584
F = 1024
EXPERTS = 256
TOPK = 8
CAP = 3
TOK_DEV = 128
TOKENS = 4096
SLOTS = 8
N_DP = 4
N_EXPERT = 8


def place_list(key):
    salted = jax.random.fold_in(key, 11)
    spare = SLOTS // 8
    primary = SLOTS - spare
    middle = 1 + jax.random.permutation(jax.random.fold_in(salted, 1), EXPERTS - 2)[:primary - 2]
    ends = jnp.array([0, EXPERTS - 1], jnp.int32)
    chosen = jnp.concatenate([ends, middle.astype(jnp.int32)])
    doubled = jax.random.permutation(jax.random.fold_in(salted, 2), primary)[:spare]
    listing = jnp.concatenate([chosen, chosen[doubled]])
    order = jax.random.permutation(jax.random.fold_in(salted, 3), SLOTS)
    return listing[order].astype(jnp.int32)


def slot_matrices(key, salt, rows, cols, fan):
    listing = place_list(key)
    salted = jax.random.fold_in(key, salt)

    def one_slot(expert):
        expert_key = jax.random.fold_in(salted, expert)
        values = jax.random.normal(expert_key, (rows, cols), jnp.float32)
        return values * fan ** (-0.5)
    return jax.vmap(one_slot)(listing)


def draw_placement(key, part):
    return place_list(key)


def draw_gate_weight(key, part):
    return slot_matrices(key, 21, D, F, D).astype(jnp.bfloat16)


def draw_up_weight(key, part):
    return slot_matrices(key, 22, D, F, D).astype(jnp.bfloat16)


def draw_down_weight(key, part):
    return slot_matrices(key, 23, F, D, F).astype(jnp.bfloat16)


def block_levels(key, extent, pieces, smallest, top_value):
    loudness, own = 1.0, jax.random.fold_in(key, 6)
    for dim, shards_of in pieces:
        draws = jnp.exp(jax.random.uniform(jax.random.fold_in(own, dim), (shards_of,), jnp.float32, smallest / len(pieces), top_value / len(pieces)))
        loudness = loudness * jnp.repeat(draws, extent[dim] // shards_of).reshape([-1 if axis == dim else 1 for axis in range(len(extent))])
    return loudness


def different_ones(own_key, rows, count, top, lift):
    order = jax.random.permutation(jax.random.fold_in(own_key, 1), count)
    pull = order
    for power in range(3):
        pull = pull * pull // count
    pull = pull * lift // count
    lots = jax.random.randint(jax.random.fold_in(own_key, 2), (rows, count), 0, 4096) + pull
    holders = jax.random.permutation(jax.random.fold_in(own_key, 3), rows)[jnp.arange(count) % rows]
    lots = jnp.where(jnp.arange(rows)[:, None] == holders[None, :], 1 << 14, lots)
    score = lots * count + jnp.arange(count)
    return lax.top_k(score.astype(jnp.int32), top)[1].astype(jnp.int32)


def normal_values(own_key, shape, spread, reach, cuts=(), kind=jnp.bfloat16):
    gain = block_levels(own_key, shape, cuts, -0.22, 0.18) if cuts else 1.0
    drawn = jax.random.normal(own_key, shape, jnp.float32) * spread * gain
    return jnp.minimum(jnp.maximum(drawn, -reach), reach).astype(kind)


def setup_inputs(seed: int = 0) -> dict:
    streams_of = jax.random.split(jax.random.key(seed), 9)
    return {
        "layer_input": normal_values(streams_of[0], (TOKENS, D), 1.0, 6.0, ((0, 32),)),
        "output_grad": normal_values(streams_of[1], (TOKENS, D), 0.3, 2.0, ((0, 32),)),
        "expert_ids": different_ones(streams_of[2], TOKENS, EXPERTS, TOPK, 512),
        "gate_probs": jnp.clip(jnp.exp(math.log(1.0) - 2.9996462 * jax.random.uniform(streams_of[3], (TOKENS, TOPK), jnp.float32) ** block_levels(streams_of[3], (TOKENS, TOPK), ((0, 32),), -0.2, 0.2)), 0.049804688, 1.0).astype(jnp.bfloat16),
        "placement": draw_placement(jax.random.fold_in(streams_of[8], 71), 0),
        "gate_weight": draw_gate_weight(jax.random.fold_in(streams_of[8], 71), 0),
        "up_weight": draw_up_weight(jax.random.fold_in(streams_of[8], 71), 0),
        "down_weight": draw_down_weight(jax.random.fold_in(streams_of[8], 71), 0),
    }


def route_table(expert_ids, placement):
    tokens_here, top_count = expert_ids.shape
    slot_count = placement.shape[0]
    matches = (expert_ids[:, :, None] == placement[None, None, :]).astype(jnp.int32)
    copies = jnp.sum(matches, axis=-1).astype(jnp.int32)
    ranking = (jnp.cumsum(matches, axis=-1) - 1).astype(jnp.int32)
    token_index = jnp.arange(tokens_here, dtype=jnp.int32)[:, None]
    pick_index = jnp.arange(top_count, dtype=jnp.int32)[None, :]
    wanted = (token_index + pick_index) % jnp.maximum(copies, 1)
    chosen = matches * (ranking == wanted[:, :, None]).astype(jnp.int32)
    flat_routes = chosen.reshape(tokens_here * top_count, slot_count)
    earlier = (jnp.cumsum(flat_routes, axis=0) - flat_routes).astype(jnp.int32)
    position = jnp.sum(earlier * flat_routes, axis=-1).astype(jnp.int32)
    routed = jnp.sum(flat_routes, axis=-1).astype(jnp.int32)
    slot_number = jnp.sum(flat_routes * jnp.arange(slot_count, dtype=jnp.int32)[None, :], axis=-1).astype(jnp.int32)
    kept = routed * (position < CAP).astype(jnp.int32)
    target = slot_number * CAP + position
    buffer_rows = jnp.arange(slot_count * CAP, dtype=jnp.int32)[:, None]
    return (buffer_rows == target[None, :]).astype(jnp.int32) * kept[None, :]


def reference(layer_input, output_grad, expert_ids, gate_probs, placement, gate_weight, up_weight, down_weight):
    blocks = N_DP * N_EXPERT
    rows_cap = SLOTS * CAP
    block_units = F // N_DP
    tables = jax.vmap(route_table, in_axes=(0, None))(expert_ids.reshape(blocks, TOK_DEV, TOPK), placement)
    token_tables = jnp.sum(tables.reshape(blocks, rows_cap, TOK_DEV, TOPK), axis=-1).astype(jnp.int32)
    source = jnp.sum(token_tables * jnp.arange(TOK_DEV, dtype=jnp.int32)[None, None, :], axis=-1).astype(jnp.int32)
    live = jnp.sum(token_tables, axis=-1).astype(jnp.int32)

    def take_rows(values):
        per_block = values.reshape(blocks, TOK_DEV, D)
        picked = jnp.take_along_axis(per_block, source[:, :, None], axis=1)
        return picked * live[:, :, None].astype(values.dtype)

    send_x = take_rows(layer_input)
    send_dy = take_rows(output_grad)
    send_w = jnp.sum(tables.astype(jnp.float32) * gate_probs.reshape(blocks, 1, TOK_DEV * TOPK).astype(jnp.float32), axis=-1).astype(jnp.bfloat16)
    slot_x = send_x.reshape(blocks, SLOTS, CAP, D).transpose(1, 0, 2, 3)
    slot_dy = send_dy.reshape(blocks, SLOTS, CAP, D).transpose(1, 0, 2, 3)
    slot_w = send_w.reshape(blocks, SLOTS, CAP).transpose(1, 0, 2)

    def per_slot(inputs):
        rows_x, rows_dy, rows_w, gate_mat, up_mat, down_mat = inputs
        flat_x = rows_x.reshape(blocks * CAP, D)
        flat_dy = rows_dy.reshape(blocks * CAP, D)
        scale = rows_w.reshape(blocks * CAP, 1).astype(jnp.float32)
        pre_gate = jnp.dot(flat_x, gate_mat, preferred_element_type=jnp.float32)
        pre_up = jnp.dot(flat_x, up_mat, preferred_element_type=jnp.float32)
        back = jnp.dot(flat_dy, down_mat.T, preferred_element_type=jnp.float32)
        sigma = jax.nn.sigmoid(pre_gate)
        active = pre_gate * sigma
        hidden = active * pre_up
        d_hidden = scale * back
        d_up = (d_hidden * active).astype(jnp.bfloat16)
        d_gate = (d_hidden * pre_up * sigma * (1.0 + pre_gate * (1.0 - sigma))).astype(jnp.bfloat16)
        scaled = (scale * hidden).astype(jnp.bfloat16)
        grad_gate_slot = jnp.dot(flat_x.T, d_gate, preferred_element_type=jnp.float32).astype(jnp.bfloat16)
        grad_up_slot = jnp.dot(flat_x.T, d_up, preferred_element_type=jnp.float32).astype(jnp.bfloat16)
        grad_down_slot = jnp.dot(scaled.T, flat_dy, preferred_element_type=jnp.float32).astype(jnp.bfloat16)
        dw_blocks = jnp.sum((hidden * back).reshape(-1, N_DP, block_units), axis=-1).astype(jnp.bfloat16)
        dw_blocks = lax.optimization_barrier(dw_blocks)
        dw_total = jnp.sum(dw_blocks.astype(jnp.float32), axis=-1).astype(jnp.bfloat16)
        gate_parts = gate_mat.reshape(D, N_DP, block_units).astype(jnp.float32)
        up_parts = up_mat.reshape(D, N_DP, block_units).astype(jnp.float32)
        dx_blocks = jnp.einsum("rjf,djf->jrd", d_gate.reshape(-1, N_DP, block_units).astype(jnp.float32), gate_parts)
        dx_blocks = dx_blocks + jnp.einsum("rjf,djf->jrd", d_up.reshape(-1, N_DP, block_units).astype(jnp.float32), up_parts)
        dx_rounded = lax.optimization_barrier(dx_blocks.astype(jnp.bfloat16))
        dx_total = jnp.sum(dx_rounded.astype(jnp.float32), axis=0).astype(jnp.bfloat16)
        return grad_gate_slot, grad_up_slot, grad_down_slot, dx_total.reshape(blocks, CAP, D), dw_total.reshape(blocks, CAP)

    outputs = lax.map(per_slot, (slot_x, slot_dy, slot_w, gate_weight, up_weight, down_weight))
    same_expert = (placement[:, None] == placement[None, :]).astype(jnp.float32)

    def replica_sum(grads):
        return jnp.einsum("st,tab->sab", same_expert, grads.astype(jnp.float32)).astype(jnp.bfloat16)

    row_dx = outputs[3].transpose(1, 0, 2, 3).reshape(blocks, rows_cap, D)
    grad_tokens = jnp.einsum("bct,bcd->btd", token_tables.astype(jnp.float32), row_dx.astype(jnp.float32))
    grad_tokens = grad_tokens.reshape(TOKENS, D).astype(jnp.bfloat16)
    row_dw = outputs[4].transpose(1, 0, 2).reshape(blocks, rows_cap)
    grad_route = jnp.einsum("bcr,bc->br", tables.astype(jnp.float32), row_dw.astype(jnp.float32))
    grad_route = grad_route.reshape(TOKENS, TOPK).astype(jnp.bfloat16)
    return grad_tokens, grad_route, replica_sum(outputs[0]), replica_sum(outputs[1]), replica_sum(outputs[2])
```

```python
import functools
import math

import jax
import jax.numpy as jnp
from jax import lax
from jax.experimental import pallas as pl
from jax.experimental.pallas import tpu as pltpu
from jax.sharding import PartitionSpec as P

MESH = pl.DeviceIdType.MESH

CAP = 3
ROWS = 8
LANES = 128
CHUNKS = 4
TILE = 256
LINES = 4


def routes(expert_ids, gate_probs, placement):
    tokens = expert_ids.shape[0]
    slots = placement.shape[0]
    ids = expert_ids.T
    probs = gate_probs.T.astype(jnp.float32)
    topk = ids.shape[0]
    same = placement[:, None] == placement[None, :]
    slot = jnp.arange(slots, dtype=jnp.int32)
    copies = jnp.sum(same.astype(jnp.int32), axis=1)
    rank = jnp.sum((same & (slot[None, :] < slot[:, None])).astype(jnp.int32), axis=1)
    turn = jnp.arange(tokens, dtype=jnp.int32)[None, :] + jnp.arange(topk, dtype=jnp.int32)[:, None]
    chosen = (ids[None] == placement[:, None, None]) & (
        turn[None] % copies[:, None, None] == rank[:, None, None]
    )
    chosen = chosen.astype(jnp.float32)
    hit = jnp.sum(chosen, axis=1)
    weight = jnp.sum(chosen * probs[None], axis=1)
    token = jnp.arange(tokens, dtype=jnp.int32)
    before = (token[:, None] < token[None, :]).astype(jnp.bfloat16)
    position = jnp.dot(hit.astype(jnp.bfloat16), before, preferred_element_type=jnp.float32)
    place = jnp.arange(CAP, dtype=jnp.float32)
    table = hit[:, None, :] * (position[:, None, :] == place[None, :, None]).astype(jnp.float32)
    row_w = jnp.sum(table * weight[:, None, :], axis=-1)
    return chosen, table, row_w, same & (slot[:, None] != slot[None, :])


def meet(groups, slots):
    d, e = lax.axis_index("dp"), lax.axis_index("expert")
    barrier = pltpu.get_barrier_semaphore()
    for k in range(1, groups):
        pl.semaphore_signal(
            barrier, inc=1, device_id=(lax.rem(d + k, groups), e), device_id_type=MESH
        )
    for k in range(1, slots):
        pl.semaphore_signal(
            barrier, inc=1, device_id=(d, lax.rem(e + k, slots)), device_id_type=MESH
        )
    pl.semaphore_wait(barrier, groups + slots - 2)


def spread_kernel(
    groups, slots, u_ref, e_ref, out_ref, landed, ready, z_send, z_recv, p_send, p_recv, own_sem
):
    d, e = lax.axis_index("dp"), lax.axis_index("expert")
    height = u_ref.shape[0]
    third = e_ref.shape[0]
    tail = ready.shape[3] - LANES
    chunk = tail // third
    meet(groups, slots)

    def onward(plane, source, way):
        return pltpu.make_async_remote_copy(
            src_ref=source,
            dst_ref=landed.at[plane],
            send_sem=z_send.at[way, plane],
            recv_sem=z_recv.at[plane],
            device_id=(d + 1 - 2 * way, e),
            device_id_type=MESH,
        )

    def across(plane, j):
        peer = lax.rem(e + j, slots)
        return pltpu.make_async_remote_copy(
            src_ref=ready.at[plane, peer],
            dst_ref=out_ref.at[plane * slots + e],
            send_sem=p_send.at[plane, j - 1],
            recv_sem=p_recv.at[plane, j - 1],
            device_id=(d, peer),
            device_id_type=MESH,
        )

    def stay(plane):
        return pltpu.make_async_copy(
            ready.at[plane, e], out_ref.at[plane * slots + e], own_sem.at[plane]
        )

    def share(plane, read):
        last = read(pl.ds(tail, chunk))
        for c in range(third):
            lanes = pl.ds(c * chunk, chunk)
            rows = jnp.dot(
                e_ref[c, :, :height], read(lanes), preferred_element_type=jnp.float32
            ) + jnp.dot(e_ref[c, :, height:], last, preferred_element_type=jnp.float32)
            for s in range(slots):
                ready[plane, s, :, lanes] = rows[s * ROWS : (s + 1) * ROWS].astype(jnp.bfloat16)
        rows = jnp.dot(
            e_ref[0, :, :height],
            read(pl.ds(tail + chunk, LANES)),
            preferred_element_type=jnp.float32,
        )
        for s in range(slots):
            ready[plane, s, :, pl.ds(tail, LANES)] = rows[s * ROWS : (s + 1) * ROWS].astype(
                jnp.bfloat16
            )
        for j in range(1, slots):
            across(plane, j).start()
        stay(plane).start()

    @pl.when(d + 1 < groups)
    def _():
        onward(d, u_ref, 0).start()

    @pl.when(d > 0)
    def _():
        onward(d, u_ref, 1).start()

    share(d, lambda lanes: u_ref[:, lanes])
    for hop in range(1, groups):
        for way in range(2):
            plane = d - hop if way == 0 else d + hop
            more = d + 1 < groups if way == 0 else d > 0
            here = plane >= 0 if way == 0 else plane < groups

            @pl.when(here)
            def _(plane=plane, more=more, way=way):
                onward(plane, landed.at[plane], way).wait_recv()

                @pl.when(more)
                def _():
                    onward(plane, landed.at[plane], way).start()

                share(plane, lambda lanes: landed[plane, :, lanes])

    for plane in range(groups):

        @pl.when((plane <= d) & (d + 1 < groups))
        def _():
            onward(plane, landed.at[plane], 0).wait_send()

        @pl.when((plane >= d) & (d > 0))
        def _():
            onward(plane, landed.at[plane], 1).wait_send()

        for j in range(1, slots):
            across(plane, j).wait()
        stay(plane).wait()


def dispatch(unique, expand, groups, slots):
    height, width = unique.shape
    packed = 3 * (width - LANES) // 4 + LANES
    landed = (groups, height, width)
    ready = (groups, slots, ROWS, packed)
    need = 2 * (math.prod(landed) + math.prod(ready) + 2 * height * width)
    return pl.pallas_call(
        functools.partial(spread_kernel, groups, slots),
        out_shape=jax.ShapeDtypeStruct((groups * slots, ROWS, packed), jnp.bfloat16),
        in_specs=[pl.BlockSpec(memory_space=pltpu.VMEM)] * 2,
        out_specs=pl.BlockSpec(memory_space=pl.ANY),
        scratch_shapes=[
            pltpu.VMEM(landed, jnp.bfloat16),
            pltpu.VMEM(ready, jnp.bfloat16),
            pltpu.SemaphoreType.DMA((2, groups)),
            pltpu.SemaphoreType.DMA((groups,)),
            pltpu.SemaphoreType.DMA((groups, slots - 1)),
            pltpu.SemaphoreType.DMA((groups, slots - 1)),
            pltpu.SemaphoreType.DMA((groups,)),
        ],
        compiler_params=pltpu.CompilerParams(
            collective_id=0, has_side_effects=True, vmem_limit_bytes=need + 8 * 2**20
        ),
    )(unique, expand)


def arrival_order(groups):
    return sorted(range(1, groups), key=lambda k: (-min(k, groups - k), k))


def fold_kernel(
    groups, slots, p_ref, e_ref, out_ref, landed, sums, z_send, z_recv, p_send, p_recv, own_sem
):
    d, e = lax.axis_index("dp"), lax.axis_index("expert")
    width = p_ref.shape[2]
    step = (width // LANES // CHUNKS) * LANES
    cuts = [pl.ds(c * step, step if c < CHUNKS - 1 else width - c * step) for c in range(CHUNKS)]
    meet(groups, slots)
    along, moved = [], []
    for c, lanes in enumerate(cuts):
        for k in arrival_order(groups):
            plane = lax.rem(d + k, groups)
            copy = pltpu.make_async_remote_copy(
                src_ref=p_ref.at[plane, :, lanes],
                dst_ref=landed.at[k - 1, :, lanes],
                send_sem=z_send.at[c, k - 1],
                recv_sem=z_recv.at[c, k - 1],
                device_id=(plane, e),
                device_id_type=MESH,
            )
            copy.start()
            along.append((c, copy))
    for c, lanes in enumerate(cuts):
        for owner, copy in along:
            if owner == c:
                copy.wait_recv()
        total = p_ref[d, :, lanes].astype(jnp.float32)
        for k in range(1, groups):
            total = total + landed[k - 1, :, lanes].astype(jnp.float32)
        rows = jnp.dot(e_ref[...], total.astype(jnp.bfloat16), preferred_element_type=jnp.float32)
        for s in range(slots):
            sums[s, :, lanes] = rows[s * ROWS : (s + 1) * ROWS].astype(jnp.bfloat16)
        for j in range(1, slots):
            peer = lax.rem(e + j, slots)
            copy = pltpu.make_async_remote_copy(
                src_ref=sums.at[peer, :, lanes],
                dst_ref=out_ref.at[e, :, lanes],
                send_sem=p_send.at[c, j - 1],
                recv_sem=p_recv.at[c, j - 1],
                device_id=(d, peer),
                device_id_type=MESH,
            )
            copy.start()
            moved.append(copy)
    kept = pltpu.make_async_copy(sums.at[e], out_ref.at[e], own_sem)
    kept.start()
    for _, copy in along:
        copy.wait_send()
    for copy in moved:
        copy.wait()
    kept.wait()


def combine(partial, expand, groups, slots):
    _, height, width = partial.shape
    need = 2 * (2 * groups * height * width + slots * ROWS * width)
    return pl.pallas_call(
        functools.partial(fold_kernel, groups, slots),
        out_shape=jax.ShapeDtypeStruct((slots, ROWS, width), jnp.bfloat16),
        in_specs=[pl.BlockSpec(memory_space=pltpu.VMEM)] * 2,
        out_specs=pl.BlockSpec(memory_space=pl.ANY),
        scratch_shapes=[
            pltpu.VMEM((groups - 1, height, width), jnp.bfloat16),
            pltpu.VMEM((slots, ROWS, width), jnp.bfloat16),
            pltpu.SemaphoreType.DMA((CHUNKS, groups - 1)),
            pltpu.SemaphoreType.DMA((CHUNKS, groups - 1)),
            pltpu.SemaphoreType.DMA((CHUNKS, slots - 1)),
            pltpu.SemaphoreType.DMA((CHUNKS, slots - 1)),
            pltpu.SemaphoreType.DMA,
        ],
        compiler_params=pltpu.CompilerParams(
            collective_id=1, has_side_effects=True, vmem_limit_bytes=need + 8 * 2**20
        ),
    )(partial, expand)


def expert_kernel(
    a_ref, gate_ref, up_ref, down_ref, gg_ref, gu_ref, gd_ref, part_ref, g_ref, du_ref, sc_ref
):
    count = a_ref.shape[0]
    width, units = gate_ref.shape
    packed = a_ref.shape[1] - LANES
    rest = packed // CAP
    own_rows = TILE // ROWS * CAP
    over_units = (((1,), (1,)), ((), ()))
    over_rows = (((0,), (0,)), ((), ()))

    @pl.loop(0, count // TILE)
    def _(t):
        here = pl.ds(pl.multiple_of(t * TILE, TILE), TILE)
        row = lax.broadcasted_iota(jnp.int32, (TILE, TILE), 0)
        col = lax.broadcasted_iota(jnp.int32, (TILE, TILE), 1)
        place = row % ROWS
        source = row - place + 2 * CAP + (place >= CAP).astype(jnp.int32)
        tail = jnp.zeros((TILE, rest), jnp.float32)
        for c in range(CAP):
            pick = (col == source) & (place < 2 * CAP) & (place % CAP == c)
            tail = tail + jnp.dot(
                pick.astype(jnp.float32).astype(jnp.bfloat16),
                a_ref[here, c * rest : (c + 1) * rest],
                preferred_element_type=jnp.float32,
            )
        g_ref[here, : packed - width] = a_ref[here, width:packed]
        g_ref[here, packed - width :] = tail.astype(jnp.bfloat16)
        flat_x = a_ref[here, :width]
        scale = a_ref[here, packed : packed + LANES].astype(jnp.float32)[:, :1]
        pre_gate = jnp.dot(flat_x, gate_ref[...], preferred_element_type=jnp.float32)
        pre_up = jnp.dot(flat_x, up_ref[...], preferred_element_type=jnp.float32)
        back = lax.dot_general(
            g_ref[here, :], down_ref[...], over_units, preferred_element_type=jnp.float32
        )
        sigma = jax.nn.sigmoid(pre_gate)
        active = pre_gate * sigma
        hidden = active * pre_up
        d_hidden = scale * back
        unit_row = lax.broadcasted_iota(jnp.int32, (TILE, units), 0)
        real = unit_row % ROWS < 2 * CAP

        def masked(values):
            return jnp.where(real, values, 0.0)

        d_up = masked(d_hidden * active).astype(jnp.bfloat16)
        d_gate = masked(d_hidden * pre_up * sigma * (1.0 + pre_gate * (1.0 - sigma))).astype(
            jnp.bfloat16
        )
        du_ref[here, :units] = d_gate
        du_ref[here, units:] = d_up
        sc_ref[here, :] = masked(scale * hidden).astype(jnp.bfloat16)
        part_dw = jnp.sum(masked(hidden * back), axis=1, keepdims=True)
        part_dw = jnp.broadcast_to(part_dw, (TILE, LANES)).astype(jnp.bfloat16)
        target = lax.broadcasted_iota(jnp.int32, (own_rows, TILE), 0)
        origin = lax.broadcasted_iota(jnp.int32, (own_rows, TILE), 1)
        keep = (origin == target // CAP * ROWS + target % CAP).astype(jnp.float32)
        keep = keep.astype(jnp.bfloat16)

        def own(values):
            return jnp.dot(keep, values, preferred_element_type=jnp.float32).astype(jnp.bfloat16)

        own_gate, own_up = own(d_gate), own(d_up)
        out = pl.ds(pl.multiple_of(t * own_rows, 8), own_rows)
        part = lax.dot_general(
            own_gate, gate_ref[...], over_units, preferred_element_type=jnp.float32
        ) + lax.dot_general(own_up, up_ref[...], over_units, preferred_element_type=jnp.float32)
        part_ref[out, :width] = part.astype(jnp.bfloat16)
        part_ref[out, width:] = own(part_dw)

    step = width // 7

    @pl.loop(0, 7)
    def _(c):
        lanes = pl.ds(pl.multiple_of(c * step, LANES), step)
        both = lax.dot_general(
            a_ref[:, lanes], du_ref[...], over_rows, preferred_element_type=jnp.float32
        )
        gg_ref[lanes, :] = both[:, :units].astype(jnp.bfloat16)
        gu_ref[lanes, :] = both[:, units:].astype(jnp.bfloat16)
        down = lax.dot_general(
            sc_ref[...], g_ref[:, lanes], over_rows, preferred_element_type=jnp.float32
        )
        gd_ref[:, lanes] = down.astype(jnp.bfloat16)


def expert_step(arrived, gate_block, up_block, down_block):
    count, packed = arrived.shape
    width, units = gate_block.shape
    part = (count // ROWS * CAP, width + LANES)
    need = 2 * (
        count * (packed + width + 3 * units) + 6 * width * units + part[0] * part[1]
    )
    shape = functools.partial(jax.ShapeDtypeStruct, dtype=jnp.bfloat16)
    return pl.pallas_call(
        expert_kernel,
        out_shape=(
            shape((width, units)),
            shape((width, units)),
            shape((units, width)),
            shape(part),
        ),
        in_specs=[pl.BlockSpec(memory_space=pltpu.VMEM)] * 4,
        out_specs=tuple([pl.BlockSpec(memory_space=pltpu.VMEM)] * 4),
        scratch_shapes=[
            pltpu.VMEM((count, width), jnp.bfloat16),
            pltpu.VMEM((count, 2 * units), jnp.bfloat16),
            pltpu.VMEM((count, units), jnp.bfloat16),
        ],
        compiler_params=pltpu.CompilerParams(
            vmem_limit_bytes=min(need + 16 * 2**20, 63 * 2**20)
        ),
    )(arrived, gate_block, up_block, down_block)


def on_device(
    layer_input, output_grad, expert_ids, gate_probs, placement, gate_weight, up_weight, down_weight
):
    slots = lax.axis_size("expert")
    groups = lax.axis_size("dp")
    tokens, width = layer_input.shape
    blocks = slots * groups
    chosen, table, row_w, twin = routes(expert_ids, gate_probs, placement)
    token_table = table.reshape(slots * CAP, tokens).astype(jnp.bfloat16)
    send_x = jnp.dot(token_table, layer_input, preferred_element_type=jnp.float32)
    send_g = jnp.dot(token_table, output_grad, preferred_element_type=jnp.float32)
    unique = jnp.concatenate(
        [send_x, send_g, jnp.broadcast_to(row_w.reshape(slots * CAP, 1), (slots * CAP, LANES))],
        axis=1,
    ).astype(jnp.bfloat16)

    row = jnp.arange(ROWS, dtype=jnp.int32)
    cap = jnp.arange(CAP, dtype=jnp.int32)
    eye = jnp.eye(slots, dtype=jnp.float32)[:, None, :, None]
    others = twin.astype(jnp.float32)[:, None, :, None]

    def layout(pick_mine, pick_theirs):
        spread = eye * pick_mine[None, :, None, :] + others * pick_theirs[None, :, None, :]
        return spread.reshape(slots * ROWS, slots * CAP)

    mine = (row[:, None] == cap[None, :]).astype(jnp.float32)
    theirs = (row[:, None] == cap[None, :] + CAP).astype(jnp.float32)
    main = layout(mine, theirs)
    expand = jnp.stack(
        [
            jnp.concatenate(
                [
                    main,
                    layout(
                        ((row[:, None] == 2 * CAP) & (cap[None, :] == c)).astype(jnp.float32),
                        ((row[:, None] == 2 * CAP + 1) & (cap[None, :] == c)).astype(jnp.float32),
                    ),
                ],
                axis=1,
            )
            for c in range(CAP)
        ]
    ).astype(jnp.bfloat16)

    arrived = dispatch(unique, expand, groups, slots)
    grad_gate, grad_up, grad_down, partial = expert_step(
        arrived.reshape(blocks * ROWS, arrived.shape[2]),
        gate_weight[0],
        up_weight[0],
        down_weight[0],
    )
    partial = partial.reshape(groups, slots * CAP, width + LANES)
    spread = (eye * mine[None, :, None, :]).reshape(slots * ROWS, slots * CAP).astype(jnp.bfloat16)
    back_rows = combine(partial, spread, groups, slots).reshape(slots * ROWS, width + LANES)

    wide = jnp.einsum("rc,sct->srt", mine, table).reshape(slots * ROWS, tokens).astype(jnp.bfloat16)
    grad_tokens = lax.dot_general(
        wide, back_rows[:, :width], (((0,), (0,)), ((), ())), preferred_element_type=jnp.float32
    ).astype(jnp.bfloat16)
    row_dw = back_rows[:, width].astype(jnp.float32)
    slot_dw = jnp.sum(
        (wide.astype(jnp.float32) * row_dw[:, None]).reshape(slots, ROWS, tokens), axis=1
    )
    grad_route = jnp.sum(chosen * slot_dw[:, None, :], axis=0).T.astype(jnp.bfloat16)
    return (
        grad_tokens,
        grad_route,
        grad_gate[None],
        grad_up[None],
        grad_down[None],
    )


def swap(count):
    row = lax.broadcasted_iota(jnp.int32, (count, count), 0)
    col = lax.broadcasted_iota(jnp.int32, (count, count), 1)
    return (col == row % 8 * 8 + row // 8).astype(jnp.float32).astype(jnp.bfloat16)


def one_hot_dot(table, values):
    return jnp.dot(table, values, preferred_element_type=jnp.float32)


def pick(place_ref, ids, slots):
    held = [place_ref[s] for s in range(slots)]
    turn = lax.broadcasted_iota(jnp.int32, ids.shape, 0) + lax.broadcasted_iota(
        jnp.int32, ids.shape, 1
    )
    chosen = []
    for s in range(slots):
        same = [(held[s] == held[q]).astype(jnp.int32) for q in range(slots)]
        copies, rank = sum(same), sum(same[:s], jnp.int32(0))
        chosen.append(
            ((ids == held[s]) & ((turn & (copies - 1)) == rank)).astype(jnp.float32)
        )
    return chosen


def tables(chosen):
    hit = jnp.concatenate([jnp.sum(c, axis=0, keepdims=True) for c in chosen], axis=0)
    tokens = hit.shape[1]
    row = lax.broadcasted_iota(jnp.int32, (tokens, tokens), 0)
    col = lax.broadcasted_iota(jnp.int32, (tokens, tokens), 1)
    before = (row < col).astype(jnp.float32).astype(jnp.bfloat16)
    position = one_hot_dot(hit.astype(jnp.bfloat16), before)
    return [jnp.where(position == float(r), hit, 0.0) for r in range(CAP)]


def stack(parts):
    return jnp.concatenate([*parts, jnp.zeros_like(parts[0])], axis=0)


def twin_of(place_ref, slots, e):
    mine = jnp.int32(0)
    for s in range(slots):
        mine = jnp.where(e == s, place_ref[s], mine)
    found, other = jnp.int32(0), jnp.int32(0)
    for s in range(slots):
        same = ((place_ref[s] == mine) & (e != s)).astype(jnp.int32)
        found = found + same
        other = other + same * s
    return found > 0, other


def exchange_kernel(
    groups,
    slots,
    place_hbm,
    ids_hbm,
    probs_hbm,
    x_hbm,
    g_hbm,
    gate_hbm,
    up_hbm,
    down_hbm,
    xs_ref,
    gs_ref,
    du_ref,
    sc_ref,
    back_ref,
    place_ref,
    ids_ref,
    probs_ref,
    x_v,
    g_v,
    gate_v,
    up_v,
    down_v,
    packed,
    landed,
    partner,
    export,
    xin,
    onward,
    yin,
    twins,
    parts,
    agg,
    total,
    ret,
    load_sem,
    a_send,
    a_recv,
    z_send,
    z_recv,
    c_send,
    c_recv,
    x_send,
    x_recv,
    y_send,
    y_recv,
    t_send,
    t_recv,
    f_send,
    f_recv,
    r_send,
    r_recv,
    own_sem,
):
    d, e = lax.axis_index("dp"), lax.axis_index("expert")
    core, ex, ey = e % 2, e // 2 % 2, e // 4
    to_core, to_x, to_y = e + 1 - 2 * core, e + 2 - 4 * ex, e + 4 - 8 * ey
    last = groups - 1
    width = x_v.shape[1]
    piece = 2 * width // 8
    units = gate_v.shape[1]
    count = parts.shape[1]
    over_units = (((1,), (1,)), ((), ()))
    half = pl.ds(core * 4, 4)
    rest = pl.ds(4 - core * 4, 4)

    get_x = pltpu.make_async_copy(x_hbm, x_v, load_sem.at[0])
    get_g = pltpu.make_async_copy(g_hbm, g_v, load_sem.at[1])
    get_w = [
        pltpu.make_async_copy(gate_hbm, gate_v, load_sem.at[2]),
        pltpu.make_async_copy(up_hbm, up_v, load_sem.at[3]),
        pltpu.make_async_copy(down_hbm, down_v, load_sem.at[4]),
    ]
    get_routes = [
        pltpu.make_async_copy(place_hbm, place_ref, load_sem.at[5]),
        pltpu.make_async_copy(ids_hbm, ids_ref, load_sem.at[6]),
        pltpu.make_async_copy(probs_hbm, probs_ref, load_sem.at[7]),
    ]
    for copy in (*get_routes, get_x, get_g):
        copy.start()
    barrier = pltpu.get_barrier_semaphore()

    @pl.when(d < last)
    def _():
        pl.semaphore_signal(barrier, inc=1, device_id=(d + 1, e), device_id_type=MESH)

    @pl.when(d > 0)
    def _():
        pl.semaphore_signal(barrier, inc=1, device_id=(d - 1, e), device_id_type=MESH)

    for k in range(1, slots):
        pl.semaphore_signal(
            barrier, inc=1, device_id=(d, lax.rem(e + k, slots)), device_id_type=MESH
        )
    for copy in get_routes:
        copy.wait()
    chosen = pick(place_ref, ids_ref[...], slots)
    table = tables(chosen)
    probs = probs_ref[...].astype(jnp.float32)
    weight = jnp.concatenate(
        [jnp.sum(c * probs, axis=0, keepdims=True) for c in chosen], axis=0
    )
    plain = stack(table).astype(jnp.bfloat16)
    scaled = stack([t * weight for t in table]).astype(jnp.bfloat16)
    turned = swap(8 * slots)
    get_x.wait()
    get_g.wait()
    for copy in get_w:
        copy.start()
    whole = [
        one_hot_dot(plain if j < 4 else scaled, source[:, j % 4 * piece : (j % 4 + 1) * piece])
        for j, source in enumerate([x_v] * 4 + [g_v] * 4)
    ]
    for r in range(CAP):
        gathered = jnp.concatenate([rows[r * 8 : (r + 1) * 8] for rows in whole], axis=0)
        moved = one_hot_dot(turned, gathered.astype(jnp.bfloat16))
        for s in range(slots):
            packed[s, :, r * piece : (r + 1) * piece] = moved[s * 8 : (s + 1) * 8].astype(
                jnp.bfloat16
            )
    pl.semaphore_wait(barrier, slots - 1 + (d > 0).astype(jnp.int32) + (d < last).astype(jnp.int32))

    def across(j):
        peer = lax.rem(e + j, slots)
        return pltpu.make_async_remote_copy(
            src_ref=packed.at[peer],
            dst_ref=landed.at[d, e],
            send_sem=a_send.at[j - 1],
            recv_sem=a_recv.at[e],
            device_id=(d, peer),
            device_id_type=MESH,
        )

    def arrival(b):
        return pltpu.make_async_remote_copy(
            src_ref=packed.at[b],
            dst_ref=landed.at[d, b],
            send_sem=a_send.at[0],
            recv_sem=a_recv.at[b],
            device_id=(d, b),
            device_id_type=MESH,
        )

    def along(plane, q, way):
        part = landed.at[plane, pl.ds(2 * q, 2)]
        return pltpu.make_async_remote_copy(
            src_ref=part,
            dst_ref=part,
            send_sem=z_send.at[way, plane, q],
            recv_sem=z_recv.at[plane, q],
            device_id=(d + 1 - 2 * way, e),
            device_id_type=MESH,
        )

    for j in range(1, slots):
        across(j).start()
    landed[d, e] = packed[e]
    for i in range(4):
        q = (ey + i // 2) % 2 * 2 + (ex + i % 2) % 2
        for b in (2 * q, 2 * q + 1):

            @pl.when(b != e)
            def _(b=b):
                arrival(b).wait_recv()

        @pl.when(d < last)
        def _(q=q):
            along(d, q, 0).start()

        @pl.when(d > 0)
        def _(q=q):
            along(d, q, 1).start()

    has, other = twin_of(place_ref, slots, e)
    core_has, core_other = twin_of(place_ref, slots, to_core)
    mine_out = has & (other // 2 != e // 2)
    core_out = core_has & (core_other // 2 != e // 2)
    target = jnp.where(mine_out, other, core_other) // 2
    from_x = target == to_x // 2

    def choose(first, a, b):
        keep = jnp.full(a.shape, first.astype(jnp.int32)) == 1
        return jnp.where(keep, a.astype(jnp.float32), b.astype(jnp.float32)).astype(jnp.bfloat16)

    def link(source, target_ref, sems, plane, device):
        return pltpu.make_async_remote_copy(
            src_ref=source,
            dst_ref=target_ref,
            send_sem=sems[0].at[plane],
            recv_sem=sems[1].at[plane],
            device_id=(d, device),
            device_id_type=MESH,
        )

    def core_copy(plane):
        return link(landed.at[plane], partner.at[plane], (c_send, c_recv), plane, to_core)

    def x_copy(plane):
        return link(export.at[plane], xin.at[plane], (x_send, x_recv), plane, to_x)

    def y_copy(plane):
        return link(onward.at[plane], yin.at[plane], (y_send, y_recv), plane, to_y)

    def half_copy(plane):
        part = twins.at[plane, half]
        return link(part, part, (t_send, t_recv), plane, to_core)

    def half_arrival(plane):
        part = twins.at[plane, rest]
        return link(part, part, (t_send, t_recv), plane, to_core)

    def relay_x(plane):
        core_copy(plane).wait_recv()
        for b in range(4):
            export[plane, b] = choose(
                mine_out, landed[plane, core * 4 + b], partner[plane, core * 4 + b]
            )
        x_copy(plane).start()

    def relay_y(plane):
        x_copy(plane).wait_recv()
        for b in range(4):
            onward[plane, b] = choose(mine_out | core_out, export[plane, b], xin[plane, b])
        y_copy(plane).start()

    def relay_half(plane):
        y_copy(plane).wait_recv()
        for b in range(4):
            twins[plane, core * 4 + b] = choose(from_x, xin[plane, b], yin[plane, b])
        half_copy(plane).start()

    def unpack(base, block):
        stacked = jnp.concatenate(
            [block(b).astype(jnp.float32) for b in range(8)], axis=0
        ).astype(jnp.bfloat16)
        moved = [
            one_hot_dot(turned, stacked[:, r * piece : (r + 1) * piece]) for r in range(CAP)
        ]
        for j in range(8):
            rows = stack([m[j * 8 : (j + 1) * 8] for m in moved]).astype(jnp.bfloat16)
            if j < 4:
                xs_ref[pl.ds(base, 32), j * piece : (j + 1) * piece] = rows
            else:
                gs_ref[pl.ds(base, 32), (j - 4) * piece : (j - 3) * piece] = rows

    def hidden_grads(base):
        rows_x = xs_ref[pl.ds(base, 32), :]
        rows_g = gs_ref[pl.ds(base, 32), :]
        pre_gate = jnp.dot(rows_x, gate_v[...], preferred_element_type=jnp.float32)
        pre_up = jnp.dot(rows_x, up_v[...], preferred_element_type=jnp.float32)
        back = lax.dot_general(
            rows_g, down_v[...], over_units, preferred_element_type=jnp.float32
        )
        sigma = jax.nn.sigmoid(pre_gate)
        active = pre_gate * sigma
        hidden = active * pre_up
        d_up = (back * active).astype(jnp.bfloat16)
        d_gate = (back * pre_up * sigma * (1.0 + pre_gate * (1.0 - sigma))).astype(jnp.bfloat16)
        du_ref[pl.ds(base, 32), :units] = d_gate
        du_ref[pl.ds(base, 32), units:] = d_up
        sc_ref[pl.ds(base, 32), :] = hidden.astype(jnp.bfloat16)
        return d_gate, d_up, jnp.sum(hidden * back, axis=1, keepdims=True)

    def own_rows(plane):
        base = pl.multiple_of(plane * 32, 32)
        unpack(base, lambda b: landed[plane, b])
        d_gate, d_up, part_dw = hidden_grads(base)
        part = lax.dot_general(
            d_gate, gate_v[...], over_units, preferred_element_type=jnp.float32
        ) + lax.dot_general(d_up, up_v[...], over_units, preferred_element_type=jnp.float32)
        part_dw = jnp.broadcast_to(part_dw, (32, LANES))
        for c in range(count):
            column = part[:, c * LANES : (c + 1) * LANES] if c < count - 1 else part_dw
            for r in range(CAP):
                parts[plane, c, r] = column[r * 8 : (r + 1) * 8].astype(jnp.bfloat16)

    def twin_rows(plane):
        base = pl.multiple_of(groups * 32 + plane * 32, 32)

        def block(b):
            near = partner[plane, b].astype(jnp.float32)
            far = twins[plane, b].astype(jnp.float32)
            take_far = jnp.full(near.shape, mine_out.astype(jnp.int32)) == 1
            take_any = jnp.full(near.shape, has.astype(jnp.int32)) == 1
            return jnp.where(take_any, jnp.where(take_far, far, near), 0.0)

        unpack(base, block)
        hidden_grads(base)

    cuts = [count * l // LINES for l in range(LINES + 1)]
    cuts = [pl.ds(a, b - a) for a, b in zip(cuts[:-1], cuts[1:])]

    def home(way, plane, l):
        return pltpu.make_async_remote_copy(
            src_ref=parts.at[plane, cuts[l]],
            dst_ref=agg.at[way, plane, cuts[l]],
            send_sem=f_send.at[plane, l],
            recv_sem=f_recv.at[way, plane, l],
            device_id=(d + 1 - 2 * way, e),
            device_id_type=MESH,
        )

    def pass_on(way, plane, l):
        home(way, plane, l).wait_recv()
        both = parts[plane, cuts[l]].astype(jnp.float32) + agg[way, plane, cuts[l]].astype(
            jnp.float32
        )
        parts[plane, cuts[l]] = both.astype(jnp.bfloat16)
        home(way, plane, l).start()

    def finish():
        total[...] = parts[d].astype(jnp.float32)
        for way in range(2):

            @pl.when(d > 0 if way == 0 else d < last)
            def _(way=way):
                for l in range(LINES):
                    home(way, d, l).wait_recv()
                total[...] = total[...] + agg[way, d].astype(jnp.float32)

        columns = []
        for k in range(ret.shape[2] // LANES):
            tall = []
            for j in range(8):
                r, c = divmod(8 * k + j, count)
                tall.append(
                    total[c, r]
                    if r < CAP
                    else jnp.zeros((8, LANES), jnp.float32)
                )
            columns.append(jnp.concatenate(tall, axis=0))
        moved = one_hot_dot(turned, jnp.concatenate(columns, axis=1).astype(jnp.bfloat16))
        for s in range(slots):
            ret[s] = moved[s * 8 : (s + 1) * 8].astype(jnp.bfloat16)
        for j in range(1, slots):
            back_copy(j).start()
        kept().start()

    def back_copy(j):
        peer = lax.rem(e + j, slots)
        return pltpu.make_async_remote_copy(
            src_ref=ret.at[peer],
            dst_ref=back_ref.at[e],
            send_sem=r_send.at[j - 1],
            recv_sem=r_recv.at[j - 1],
            device_id=(d, peer),
            device_id_type=MESH,
        )

    def kept():
        return pltpu.make_async_copy(ret.at[e], back_ref.at[e], own_sem)

    middle = (d > 0).astype(jnp.int32) * (d < last).astype(jnp.int32)
    sign = 1 - 2 * (d // 2)

    def nth(n):
        return d + sign * (n - middle * ((n + 3) // 4) * ((5 - n) // 2))

    def hop_arrives(hop):
        for q in range(4):
            for way in range(2):
                plane = d - hop if way == 0 else d + hop
                more = d < last if way == 0 else d > 0

                @pl.when(plane >= 0 if way == 0 else plane <= last)
                def _(plane=plane, more=more, way=way):
                    along(plane, q, way).wait_recv()

                    @pl.when(more)
                    def _():
                        along(plane, q, way).start()

    for copy in get_w:
        copy.wait()

    @pl.loop(0, groups)
    def _(n):
        @pl.when((n > 0) & ((middle == 0) | (n != 2)))
        def _():
            hop_arrives(n - middle * (n // 3))

        plane = nth(n)
        core_copy(plane).start()
        own_rows(plane)

        @pl.when((middle == 0) & (n > 0))
        def _():
            for l in range(LINES):
                for way in range(2):

                    @pl.when(plane > d if way == 0 else plane < d)
                    def _(way=way):
                        home(way, plane, l).start()

        relay_x(plane)

        @pl.when(n > 0)
        def _():
            relay_y(nth(n - 1))

        @pl.when(n > 1)
        def _():
            relay_half(nth(n - 2))

    relay_y(nth(3))

    @pl.when(middle == 1)
    def _():
        for way in range(2):

            @pl.when(d == 1 + way)
            def _(way=way):
                for l in range(LINES):
                    pass_on(way, 2 - way, l)

        finish()

    relay_half(nth(2))
    relay_half(nth(3))

    @pl.loop(0, groups)
    def _(n):
        plane = nth(n)
        half_arrival(plane).wait_recv()
        twin_rows(plane)

    @pl.when(middle == 1)
    def _():
        for way in range(2):

            @pl.when(d == 1 + way)
            def _(way=way):
                for l in range(LINES):
                    pass_on(way, last * (1 - way), l)
                for l in range(LINES):
                    pass_on(1 - way, last * way, l)

    @pl.when(middle == 0)
    def _():
        finish()

    for j in range(1, slots):
        across(j).wait_send()
        back_copy(j).wait()
    kept().wait()
    for plane in range(groups):
        for q in range(4):

            @pl.when((plane <= d) & (d < last))
            def _(plane=plane, q=q):
                along(plane, q, 0).wait_send()

            @pl.when((plane >= d) & (d > 0))
            def _(plane=plane, q=q):
                along(plane, q, 1).wait_send()

        core_copy(plane).wait_send()
        x_copy(plane).wait_send()
        y_copy(plane).wait_send()
        half_copy(plane).wait_send()
        for l in range(LINES):
            for way in range(2):

                @pl.when(plane > d if way == 0 else plane < d)
                def _(plane=plane, way=way, l=l):
                    home(way, plane, l).wait_send()


def exchange(ids, probs, placement, x, g, gate, up, down, groups, slots):
    tokens, width = x.shape
    units = gate.shape[1]
    piece = width // 4
    full = width + LANES
    back = pl.cdiv(CAP * full, 8 * LANES) * LANES
    rows = 2 * groups * 32
    bf16 = jnp.bfloat16
    shape = functools.partial(jax.ShapeDtypeStruct, dtype=bf16)
    vmem, hbm = pl.BlockSpec(memory_space=pltpu.VMEM), pl.BlockSpec(memory_space=pltpu.HBM)
    dma = pltpu.SemaphoreType.DMA
    planes = (groups, 8, 8, CAP * piece)
    halves = (groups, 4, 8, CAP * piece)
    return pl.pallas_call(
        functools.partial(exchange_kernel, groups, slots),
        out_shape=(
            shape((rows, width)),
            shape((rows, width)),
            shape((rows, 2 * units)),
            shape((rows, units)),
            shape((slots, 8, back)),
        ),
        in_specs=[hbm] * 8,
        out_specs=(vmem, vmem, vmem, vmem, pl.BlockSpec(memory_space=pl.ANY)),
        scratch_shapes=[
            pltpu.SMEM(placement.shape, jnp.int32),
            pltpu.VMEM(ids.shape, jnp.int32),
            pltpu.VMEM(probs.shape, bf16),
            pltpu.VMEM((tokens, width), bf16),
            pltpu.VMEM((tokens, width), bf16),
            pltpu.VMEM((width, units), bf16),
            pltpu.VMEM((width, units), bf16),
            pltpu.VMEM((units, width), bf16),
            pltpu.VMEM((slots, 8, CAP * piece), bf16),
            pltpu.VMEM(planes, bf16),
            pltpu.VMEM(planes, bf16),
            pltpu.VMEM(halves, bf16),
            pltpu.VMEM(halves, bf16),
            pltpu.VMEM(halves, bf16),
            pltpu.VMEM(halves, bf16),
            pltpu.VMEM(planes, bf16),
            pltpu.VMEM((groups, full // LANES, CAP, 8, LANES), bf16),
            pltpu.VMEM((2, groups, full // LANES, CAP, 8, LANES), bf16),
            pltpu.VMEM((full // LANES, CAP, 8, LANES), jnp.float32),
            pltpu.VMEM((slots, 8, back), bf16),
            dma((8,)),
            dma((slots - 1,)),
            dma((slots,)),
            dma((2, groups, 4)),
            dma((groups, 4)),
            dma((groups,)),
            dma((groups,)),
            dma((groups,)),
            dma((groups,)),
            dma((groups,)),
            dma((groups,)),
            dma((groups,)),
            dma((groups,)),
            dma((groups, LINES)),
            dma((2, groups, LINES)),
            dma((slots - 1,)),
            dma((slots - 1,)),
            dma,
        ],
        compiler_params=pltpu.CompilerParams(
            collective_id=2, has_side_effects=True, vmem_limit_bytes=36 * 2**20
        ),
    )(
        *(
            pltpu.with_memory_space_constraint(value, pltpu.HBM)
            for value in (placement, ids, probs, x, g, gate, up, down)
        )
    )


def gradient_kernel(
    slots,
    place_ref,
    ids_ref,
    probs_ref,
    xs_ref,
    gs_ref,
    du_ref,
    sc_ref,
    back_ref,
    gg_hbm,
    gu_hbm,
    gd_hbm,
    tokens_hbm,
    route_ref,
    gg_v,
    gu_v,
    gd_v,
    tokens_v,
    rows_v,
    sems,
):
    width = xs_ref.shape[1]
    units = sc_ref.shape[1]
    steps = 7
    step = width // steps
    over_rows = (((0,), (0,)), ((), ()))
    copies = []
    for c in range(steps):
        lanes = pl.ds(c * step, step)
        both = lax.dot_general(
            xs_ref[:, lanes], du_ref[...], over_rows, preferred_element_type=jnp.float32
        )
        gg_v[lanes, :] = both[:, :units].astype(jnp.bfloat16)
        gu_v[lanes, :] = both[:, units:].astype(jnp.bfloat16)
        gd_v[:, lanes] = lax.dot_general(
            sc_ref[...], gs_ref[:, lanes], over_rows, preferred_element_type=jnp.float32
        ).astype(jnp.bfloat16)
        for i, (source, target) in enumerate(
            [
                (gg_v.at[lanes, :], gg_hbm.at[lanes, :]),
                (gu_v.at[lanes, :], gu_hbm.at[lanes, :]),
                (gd_v.at[:, lanes], gd_hbm.at[:, lanes]),
            ]
        ):
            copy = pltpu.make_async_copy(source, target, sems.at[c, i])
            copy.start()
            copies.append(copy)

    chosen = pick(place_ref, ids_ref[...], slots)
    table = tables(chosen)
    stacked = jnp.concatenate(
        [back_ref[s].astype(jnp.float32) for s in range(slots)], axis=0
    ).astype(jnp.bfloat16)
    moved = one_hot_dot(swap(8 * slots), stacked)
    count = rows_v.shape[1] // LANES

    def tile(r, c):
        k, j = divmod(r * count + c, 8)
        return moved[j * 8 : (j + 1) * 8, k * LANES : (k + 1) * LANES]

    for c in range(count - 1):
        rows_v[:, c * LANES : (c + 1) * LANES] = stack(
            [tile(r, c) for r in range(CAP)]
        ).astype(jnp.bfloat16)
    tokens_v[...] = lax.dot_general(
        stack(table).astype(jnp.bfloat16),
        rows_v[:, :width],
        over_rows,
        preferred_element_type=jnp.float32,
    ).astype(jnp.bfloat16)
    copy = pltpu.make_async_copy(tokens_v, tokens_hbm, sems.at[0, 3])
    copy.start()
    copies.append(copy)
    slot_dw = sum(table[r] * tile(r, count - 1) for r in range(CAP))
    route = sum(chosen[s] * slot_dw[s : s + 1] for s in range(slots))
    route_ref[...] = (route / probs_ref[...].astype(jnp.float32)).astype(jnp.bfloat16)
    for copy in copies:
        copy.wait()


def gradients(placement, ids, probs, arrived, slots, tokens):
    xs, gs, du, sc, back = arrived
    width, units = xs.shape[1], sc.shape[1]
    bf16 = jnp.bfloat16
    shape = functools.partial(jax.ShapeDtypeStruct, dtype=bf16)
    vmem, hbm = pl.BlockSpec(memory_space=pltpu.VMEM), pl.BlockSpec(memory_space=pl.ANY)
    return pl.pallas_call(
        functools.partial(gradient_kernel, slots),
        out_shape=(
            shape((width, units)),
            shape((width, units)),
            shape((units, width)),
            shape((tokens, width)),
            shape(probs.shape),
        ),
        in_specs=[pl.BlockSpec(memory_space=pltpu.SMEM)] + [vmem] * 7,
        out_specs=(hbm, hbm, hbm, hbm, vmem),
        scratch_shapes=[
            pltpu.VMEM((width, units), bf16),
            pltpu.VMEM((width, units), bf16),
            pltpu.VMEM((units, width), bf16),
            pltpu.VMEM((tokens, width), bf16),
            pltpu.VMEM((32, width + LANES), bf16),
            pltpu.SemaphoreType.DMA((7, 4)),
        ],
        compiler_params=pltpu.CompilerParams(vmem_limit_bytes=36 * 2**20),
    )(placement, ids, probs, xs, gs, du, sc, back)


def on_small_slice(
    layer_input, output_grad, expert_ids, gate_probs, placement, gate_weight, up_weight, down_weight
):
    slots = lax.axis_size("expert")
    groups = lax.axis_size("dp")
    ids, probs = expert_ids.T, gate_probs.T
    arrived = exchange(
        ids,
        probs,
        placement,
        layer_input,
        output_grad,
        gate_weight[0],
        up_weight[0],
        down_weight[0],
        groups,
        slots,
    )
    grad_gate, grad_up, grad_down, grad_tokens, grad_route = gradients(
        placement, ids, probs, arrived, slots, layer_input.shape[0]
    )
    return grad_tokens, grad_route.T, grad_gate[None], grad_up[None], grad_down[None]


def solution(mesh):
    in_specs = (
        P(("dp", "expert"), None),
        P(("dp", "expert"), None),
        P(("dp", "expert"), None),
        P(("dp", "expert"), None),
        P(),
        P("expert", None, "dp"),
        P("expert", None, "dp"),
        P("expert", "dp", None),
    )
    out_specs = (
        P(("dp", "expert"), None),
        P(("dp", "expert"), None),
        P("expert", None, "dp"),
        P("expert", None, "dp"),
        P("expert", "dp", None),
    )
    small = mesh.shape["dp"] == 4 and mesh.shape["expert"] == 8
    return jax.shard_map(
        on_small_slice if small else on_device, mesh=mesh, in_specs=in_specs, out_specs=out_specs, check_vma=False
    )
```

```python
import functools
import math

import jax
import jax.numpy as jnp
from jax import lax
from jax.experimental import pallas as pl
from jax.experimental.pallas import tpu as pltpu
from jax.sharding import PartitionSpec as P

MESH = pl.DeviceIdType.MESH

CAP = 3
ROWS = 8
LANES = 128
CHUNKS = 4
TILE = 256
LINES = 4


def routes(expert_ids, gate_probs, placement):
    tokens = expert_ids.shape[0]
    slots = placement.shape[0]
    ids = expert_ids.T
    probs = gate_probs.T.astype(jnp.float32)
    topk = ids.shape[0]
    same = placement[:, None] == placement[None, :]
    slot = jnp.arange(slots, dtype=jnp.int32)
    copies = jnp.sum(same.astype(jnp.int32), axis=1)
    rank = jnp.sum((same & (slot[None, :] < slot[:, None])).astype(jnp.int32), axis=1)
    turn = jnp.arange(tokens, dtype=jnp.int32)[None, :] + jnp.arange(topk, dtype=jnp.int32)[:, None]
    chosen = (ids[None] == placement[:, None, None]) & (
        turn[None] % copies[:, None, None] == rank[:, None, None]
    )
    chosen = chosen.astype(jnp.float32)
    hit = jnp.sum(chosen, axis=1)
    weight = jnp.sum(chosen * probs[None], axis=1)
    token = jnp.arange(tokens, dtype=jnp.int32)
    before = (token[:, None] < token[None, :]).astype(jnp.bfloat16)
    position = jnp.dot(hit.astype(jnp.bfloat16), before, preferred_element_type=jnp.float32)
    place = jnp.arange(CAP, dtype=jnp.float32)
    table = hit[:, None, :] * (position[:, None, :] == place[None, :, None]).astype(jnp.float32)
    row_w = jnp.sum(table * weight[:, None, :], axis=-1)
    return chosen, table, row_w, same & (slot[:, None] != slot[None, :])


def meet(groups, slots):
    d, e = lax.axis_index("dp"), lax.axis_index("expert")
    barrier = pltpu.get_barrier_semaphore()
    for k in range(1, groups):
        pl.semaphore_signal(
            barrier, inc=1, device_id=(lax.rem(d + k, groups), e), device_id_type=MESH
        )
    for k in range(1, slots):
        pl.semaphore_signal(
            barrier, inc=1, device_id=(d, lax.rem(e + k, slots)), device_id_type=MESH
        )
    pl.semaphore_wait(barrier, groups + slots - 2)


def spread_kernel(
    groups, slots, u_ref, e_ref, out_ref, landed, ready, z_send, z_recv, p_send, p_recv, own_sem
):
    d, e = lax.axis_index("dp"), lax.axis_index("expert")
    height = u_ref.shape[0]
    third = e_ref.shape[0]
    tail = ready.shape[3] - LANES
    chunk = tail // third
    meet(groups, slots)

    def onward(plane, source, way):
        return pltpu.make_async_remote_copy(
            src_ref=source,
            dst_ref=landed.at[plane],
            send_sem=z_send.at[way, plane],
            recv_sem=z_recv.at[plane],
            device_id=(d + 1 - 2 * way, e),
            device_id_type=MESH,
        )

    def across(plane, j):
        peer = lax.rem(e + j, slots)
        return pltpu.make_async_remote_copy(
            src_ref=ready.at[plane, peer],
            dst_ref=out_ref.at[plane * slots + e],
            send_sem=p_send.at[plane, j - 1],
            recv_sem=p_recv.at[plane, j - 1],
            device_id=(d, peer),
            device_id_type=MESH,
        )

    def stay(plane):
        return pltpu.make_async_copy(
            ready.at[plane, e], out_ref.at[plane * slots + e], own_sem.at[plane]
        )

    def share(plane, read):
        last = read(pl.ds(tail, chunk))
        for c in range(third):
            lanes = pl.ds(c * chunk, chunk)
            rows = jnp.dot(
                e_ref[c, :, :height], read(lanes), preferred_element_type=jnp.float32
            ) + jnp.dot(e_ref[c, :, height:], last, preferred_element_type=jnp.float32)
            for s in range(slots):
                ready[plane, s, :, lanes] = rows[s * ROWS : (s + 1) * ROWS].astype(jnp.bfloat16)
        rows = jnp.dot(
            e_ref[0, :, :height],
            read(pl.ds(tail + chunk, LANES)),
            preferred_element_type=jnp.float32,
        )
        for s in range(slots):
            ready[plane, s, :, pl.ds(tail, LANES)] = rows[s * ROWS : (s + 1) * ROWS].astype(
                jnp.bfloat16
            )
        for j in range(1, slots):
            across(plane, j).start()
        stay(plane).start()

    @pl.when(d + 1 < groups)
    def _():
        onward(d, u_ref, 0).start()

    @pl.when(d > 0)
    def _():
        onward(d, u_ref, 1).start()

    share(d, lambda lanes: u_ref[:, lanes])
    for hop in range(1, groups):
        for way in range(2):
            plane = d - hop if way == 0 else d + hop
            more = d + 1 < groups if way == 0 else d > 0
            here = plane >= 0 if way == 0 else plane < groups

            @pl.when(here)
            def _(plane=plane, more=more, way=way):
                onward(plane, landed.at[plane], way).wait_recv()

                @pl.when(more)
                def _():
                    onward(plane, landed.at[plane], way).start()

                share(plane, lambda lanes: landed[plane, :, lanes])

    for plane in range(groups):

        @pl.when((plane <= d) & (d + 1 < groups))
        def _():
            onward(plane, landed.at[plane], 0).wait_send()

        @pl.when((plane >= d) & (d > 0))
        def _():
            onward(plane, landed.at[plane], 1).wait_send()

        for j in range(1, slots):
            across(plane, j).wait()
        stay(plane).wait()


def dispatch(unique, expand, groups, slots):
    height, width = unique.shape
    packed = 3 * (width - LANES) // 4 + LANES
    landed = (groups, height, width)
    ready = (groups, slots, ROWS, packed)
    need = 2 * (math.prod(landed) + math.prod(ready) + 2 * height * width)
    return pl.pallas_call(
        functools.partial(spread_kernel, groups, slots),
        out_shape=jax.ShapeDtypeStruct((groups * slots, ROWS, packed), jnp.bfloat16),
        in_specs=[pl.BlockSpec(memory_space=pltpu.VMEM)] * 2,
        out_specs=pl.BlockSpec(memory_space=pl.ANY),
        scratch_shapes=[
            pltpu.VMEM(landed, jnp.bfloat16),
            pltpu.VMEM(ready, jnp.bfloat16),
            pltpu.SemaphoreType.DMA((2, groups)),
            pltpu.SemaphoreType.DMA((groups,)),
            pltpu.SemaphoreType.DMA((groups, slots - 1)),
            pltpu.SemaphoreType.DMA((groups, slots - 1)),
            pltpu.SemaphoreType.DMA((groups,)),
        ],
        compiler_params=pltpu.CompilerParams(
            collective_id=0, has_side_effects=True, vmem_limit_bytes=need + 8 * 2**20
        ),
    )(unique, expand)


def arrival_order(groups):
    return sorted(range(1, groups), key=lambda k: (-min(k, groups - k), k))


def fold_kernel(
    groups, slots, p_ref, e_ref, out_ref, landed, sums, z_send, z_recv, p_send, p_recv, own_sem
):
    d, e = lax.axis_index("dp"), lax.axis_index("expert")
    width = p_ref.shape[2]
    step = (width // LANES // CHUNKS) * LANES
    cuts = [pl.ds(c * step, step if c < CHUNKS - 1 else width - c * step) for c in range(CHUNKS)]
    meet(groups, slots)
    along, moved = [], []
    for c, lanes in enumerate(cuts):
        for k in arrival_order(groups):
            plane = lax.rem(d + k, groups)
            copy = pltpu.make_async_remote_copy(
                src_ref=p_ref.at[plane, :, lanes],
                dst_ref=landed.at[k - 1, :, lanes],
                send_sem=z_send.at[c, k - 1],
                recv_sem=z_recv.at[c, k - 1],
                device_id=(plane, e),
                device_id_type=MESH,
            )
            copy.start()
            along.append((c, copy))
    for c, lanes in enumerate(cuts):
        for owner, copy in along:
            if owner == c:
                copy.wait_recv()
        total = p_ref[d, :, lanes].astype(jnp.float32)
        for k in range(1, groups):
            total = total + landed[k - 1, :, lanes].astype(jnp.float32)
        rows = jnp.dot(e_ref[...], total.astype(jnp.bfloat16), preferred_element_type=jnp.float32)
        for s in range(slots):
            sums[s, :, lanes] = rows[s * ROWS : (s + 1) * ROWS].astype(jnp.bfloat16)
        for j in range(1, slots):
            peer = lax.rem(e + j, slots)
            copy = pltpu.make_async_remote_copy(
                src_ref=sums.at[peer, :, lanes],
                dst_ref=out_ref.at[e, :, lanes],
                send_sem=p_send.at[c, j - 1],
                recv_sem=p_recv.at[c, j - 1],
                device_id=(d, peer),
                device_id_type=MESH,
            )
            copy.start()
            moved.append(copy)
    kept = pltpu.make_async_copy(sums.at[e], out_ref.at[e], own_sem)
    kept.start()
    for _, copy in along:
        copy.wait_send()
    for copy in moved:
        copy.wait()
    kept.wait()


def combine(partial, expand, groups, slots):
    _, height, width = partial.shape
    need = 2 * (2 * groups * height * width + slots * ROWS * width)
    return pl.pallas_call(
        functools.partial(fold_kernel, groups, slots),
        out_shape=jax.ShapeDtypeStruct((slots, ROWS, width), jnp.bfloat16),
        in_specs=[pl.BlockSpec(memory_space=pltpu.VMEM)] * 2,
        out_specs=pl.BlockSpec(memory_space=pl.ANY),
        scratch_shapes=[
            pltpu.VMEM((groups - 1, height, width), jnp.bfloat16),
            pltpu.VMEM((slots, ROWS, width), jnp.bfloat16),
            pltpu.SemaphoreType.DMA((CHUNKS, groups - 1)),
            pltpu.SemaphoreType.DMA((CHUNKS, groups - 1)),
            pltpu.SemaphoreType.DMA((CHUNKS, slots - 1)),
            pltpu.SemaphoreType.DMA((CHUNKS, slots - 1)),
            pltpu.SemaphoreType.DMA,
        ],
        compiler_params=pltpu.CompilerParams(
            collective_id=1, has_side_effects=True, vmem_limit_bytes=need + 8 * 2**20
        ),
    )(partial, expand)


def expert_kernel(
    a_ref, gate_ref, up_ref, down_ref, gg_ref, gu_ref, gd_ref, part_ref, g_ref, du_ref, sc_ref
):
    count = a_ref.shape[0]
    width, units = gate_ref.shape
    packed = a_ref.shape[1] - LANES
    rest = packed // CAP
    own_rows = TILE // ROWS * CAP
    over_units = (((1,), (1,)), ((), ()))
    over_rows = (((0,), (0,)), ((), ()))

    @pl.loop(0, count // TILE)
    def _(t):
        here = pl.ds(pl.multiple_of(t * TILE, TILE), TILE)
        row = lax.broadcasted_iota(jnp.int32, (TILE, TILE), 0)
        col = lax.broadcasted_iota(jnp.int32, (TILE, TILE), 1)
        place = row % ROWS
        source = row - place + 2 * CAP + (place >= CAP).astype(jnp.int32)
        tail = jnp.zeros((TILE, rest), jnp.float32)
        for c in range(CAP):
            pick = (col == source) & (place < 2 * CAP) & (place % CAP == c)
            tail = tail + jnp.dot(
                pick.astype(jnp.float32).astype(jnp.bfloat16),
                a_ref[here, c * rest : (c + 1) * rest],
                preferred_element_type=jnp.float32,
            )
        g_ref[here, : packed - width] = a_ref[here, width:packed]
        g_ref[here, packed - width :] = tail.astype(jnp.bfloat16)
        flat_x = a_ref[here, :width]
        scale = a_ref[here, packed : packed + LANES].astype(jnp.float32)[:, :1]
        pre_gate = jnp.dot(flat_x, gate_ref[...], preferred_element_type=jnp.float32)
        pre_up = jnp.dot(flat_x, up_ref[...], preferred_element_type=jnp.float32)
        back = lax.dot_general(
            g_ref[here, :], down_ref[...], over_units, preferred_element_type=jnp.float32
        )
        sigma = jax.nn.sigmoid(pre_gate)
        active = pre_gate * sigma
        hidden = active * pre_up
        d_hidden = scale * back
        unit_row = lax.broadcasted_iota(jnp.int32, (TILE, units), 0)
        real = unit_row % ROWS < 2 * CAP

        def masked(values):
            return jnp.where(real, values, 0.0)

        d_up = masked(d_hidden * active).astype(jnp.bfloat16)
        d_gate = masked(d_hidden * pre_up * sigma * (1.0 + pre_gate * (1.0 - sigma))).astype(
            jnp.bfloat16
        )
        du_ref[here, :units] = d_gate
        du_ref[here, units:] = d_up
        sc_ref[here, :] = masked(scale * hidden).astype(jnp.bfloat16)
        part_dw = jnp.sum(masked(hidden * back), axis=1, keepdims=True)
        part_dw = jnp.broadcast_to(part_dw, (TILE, LANES)).astype(jnp.bfloat16)
        target = lax.broadcasted_iota(jnp.int32, (own_rows, TILE), 0)
        origin = lax.broadcasted_iota(jnp.int32, (own_rows, TILE), 1)
        keep = (origin == target // CAP * ROWS + target % CAP).astype(jnp.float32)
        keep = keep.astype(jnp.bfloat16)

        def own(values):
            return jnp.dot(keep, values, preferred_element_type=jnp.float32).astype(jnp.bfloat16)

        own_gate, own_up = own(d_gate), own(d_up)
        out = pl.ds(pl.multiple_of(t * own_rows, 8), own_rows)
        part = lax.dot_general(
            own_gate, gate_ref[...], over_units, preferred_element_type=jnp.float32
        ) + lax.dot_general(own_up, up_ref[...], over_units, preferred_element_type=jnp.float32)
        part_ref[out, :width] = part.astype(jnp.bfloat16)
        part_ref[out, width:] = own(part_dw)

    step = width // 7

    @pl.loop(0, 7)
    def _(c):
        lanes = pl.ds(pl.multiple_of(c * step, LANES), step)
        both = lax.dot_general(
            a_ref[:, lanes], du_ref[...], over_rows, preferred_element_type=jnp.float32
        )
        gg_ref[lanes, :] = both[:, :units].astype(jnp.bfloat16)
        gu_ref[lanes, :] = both[:, units:].astype(jnp.bfloat16)
        down = lax.dot_general(
            sc_ref[...], g_ref[:, lanes], over_rows, preferred_element_type=jnp.float32
        )
        gd_ref[:, lanes] = down.astype(jnp.bfloat16)


def expert_step(arrived, gate_block, up_block, down_block):
    count, packed = arrived.shape
    width, units = gate_block.shape
    part = (count // ROWS * CAP, width + LANES)
    need = 2 * (
        count * (packed + width + 3 * units) + 6 * width * units + part[0] * part[1]
    )
    shape = functools.partial(jax.ShapeDtypeStruct, dtype=jnp.bfloat16)
    return pl.pallas_call(
        expert_kernel,
        out_shape=(
            shape((width, units)),
            shape((width, units)),
            shape((units, width)),
            shape(part),
        ),
        in_specs=[pl.BlockSpec(memory_space=pltpu.VMEM)] * 4,
        out_specs=tuple([pl.BlockSpec(memory_space=pltpu.VMEM)] * 4),
        scratch_shapes=[
            pltpu.VMEM((count, width), jnp.bfloat16),
            pltpu.VMEM((count, 2 * units), jnp.bfloat16),
            pltpu.VMEM((count, units), jnp.bfloat16),
        ],
        compiler_params=pltpu.CompilerParams(
            vmem_limit_bytes=min(need + 16 * 2**20, 63 * 2**20)
        ),
    )(arrived, gate_block, up_block, down_block)


def on_device(
    layer_input, output_grad, expert_ids, gate_probs, placement, gate_weight, up_weight, down_weight
):
    slots = lax.axis_size("expert")
    groups = lax.axis_size("dp")
    tokens, width = layer_input.shape
    blocks = slots * groups
    chosen, table, row_w, twin = routes(expert_ids, gate_probs, placement)
    token_table = table.reshape(slots * CAP, tokens).astype(jnp.bfloat16)
    send_x = jnp.dot(token_table, layer_input, preferred_element_type=jnp.float32)
    send_g = jnp.dot(token_table, output_grad, preferred_element_type=jnp.float32)
    unique = jnp.concatenate(
        [send_x, send_g, jnp.broadcast_to(row_w.reshape(slots * CAP, 1), (slots * CAP, LANES))],
        axis=1,
    ).astype(jnp.bfloat16)

    row = jnp.arange(ROWS, dtype=jnp.int32)
    cap = jnp.arange(CAP, dtype=jnp.int32)
    eye = jnp.eye(slots, dtype=jnp.float32)[:, None, :, None]
    others = twin.astype(jnp.float32)[:, None, :, None]

    def layout(pick_mine, pick_theirs):
        spread = eye * pick_mine[None, :, None, :] + others * pick_theirs[None, :, None, :]
        return spread.reshape(slots * ROWS, slots * CAP)

    mine = (row[:, None] == cap[None, :]).astype(jnp.float32)
    theirs = (row[:, None] == cap[None, :] + CAP).astype(jnp.float32)
    main = layout(mine, theirs)
    expand = jnp.stack(
        [
            jnp.concatenate(
                [
                    main,
                    layout(
                        ((row[:, None] == 2 * CAP) & (cap[None, :] == c)).astype(jnp.float32),
                        ((row[:, None] == 2 * CAP + 1) & (cap[None, :] == c)).astype(jnp.float32),
                    ),
                ],
                axis=1,
            )
            for c in range(CAP)
        ]
    ).astype(jnp.bfloat16)

    arrived = dispatch(unique, expand, groups, slots)
    grad_gate, grad_up, grad_down, partial = expert_step(
        arrived.reshape(blocks * ROWS, arrived.shape[2]),
        gate_weight[0],
        up_weight[0],
        down_weight[0],
    )
    partial = partial.reshape(groups, slots * CAP, width + LANES)
    spread = (eye * mine[None, :, None, :]).reshape(slots * ROWS, slots * CAP).astype(jnp.bfloat16)
    back_rows = combine(partial, spread, groups, slots).reshape(slots * ROWS, width + LANES)

    wide = jnp.einsum("rc,sct->srt", mine, table).reshape(slots * ROWS, tokens).astype(jnp.bfloat16)
    grad_tokens = lax.dot_general(
        wide, back_rows[:, :width], (((0,), (0,)), ((), ())), preferred_element_type=jnp.float32
    ).astype(jnp.bfloat16)
    row_dw = back_rows[:, width].astype(jnp.float32)
    slot_dw = jnp.sum(
        (wide.astype(jnp.float32) * row_dw[:, None]).reshape(slots, ROWS, tokens), axis=1
    )
    grad_route = jnp.sum(chosen * slot_dw[:, None, :], axis=0).T.astype(jnp.bfloat16)
    return (
        grad_tokens,
        grad_route,
        grad_gate[None],
        grad_up[None],
        grad_down[None],
    )


def swap(count):
    row = lax.broadcasted_iota(jnp.int32, (count, count), 0)
    col = lax.broadcasted_iota(jnp.int32, (count, count), 1)
    return (col == row % 8 * 8 + row // 8).astype(jnp.float32).astype(jnp.bfloat16)


def one_hot_dot(table, values):
    return jnp.dot(table, values, preferred_element_type=jnp.float32)


def pick(place_ref, ids, slots):
    held = [place_ref[s] for s in range(slots)]
    turn = lax.broadcasted_iota(jnp.int32, ids.shape, 0) + lax.broadcasted_iota(
        jnp.int32, ids.shape, 1
    )
    chosen = []
    for s in range(slots):
        same = [(held[s] == held[q]).astype(jnp.int32) for q in range(slots)]
        copies, rank = sum(same), sum(same[:s], jnp.int32(0))
        chosen.append(
            ((ids == held[s]) & ((turn & (copies - 1)) == rank)).astype(jnp.float32)
        )
    return chosen


def tables(chosen):
    hit = jnp.concatenate([jnp.sum(c, axis=0, keepdims=True) for c in chosen], axis=0)
    tokens = hit.shape[1]
    row = lax.broadcasted_iota(jnp.int32, (tokens, tokens), 0)
    col = lax.broadcasted_iota(jnp.int32, (tokens, tokens), 1)
    before = (row < col).astype(jnp.float32).astype(jnp.bfloat16)
    position = one_hot_dot(hit.astype(jnp.bfloat16), before)
    return [jnp.where(position == float(r), hit, 0.0) for r in range(CAP)]


def stack(parts):
    return jnp.concatenate([*parts, jnp.zeros_like(parts[0])], axis=0)


def twin_of(place_ref, slots, e):
    mine = jnp.int32(0)
    for s in range(slots):
        mine = jnp.where(e == s, place_ref[s], mine)
    found, other = jnp.int32(0), jnp.int32(0)
    for s in range(slots):
        same = ((place_ref[s] == mine) & (e != s)).astype(jnp.int32)
        found = found + same
        other = other + same * s
    return found > 0, other


def exchange_kernel(
    groups,
    slots,
    place_hbm,
    ids_hbm,
    probs_hbm,
    x_hbm,
    g_hbm,
    gate_hbm,
    up_hbm,
    down_hbm,
    xs_ref,
    gs_ref,
    du_ref,
    sc_ref,
    back_ref,
    place_ref,
    ids_ref,
    probs_ref,
    x_v,
    g_v,
    gate_v,
    up_v,
    down_v,
    packed,
    landed,
    partner,
    export,
    xin,
    onward,
    yin,
    twins,
    parts,
    agg,
    total,
    ret,
    load_sem,
    a_send,
    a_recv,
    z_send,
    z_recv,
    c_send,
    c_recv,
    x_send,
    x_recv,
    y_send,
    y_recv,
    t_send,
    t_recv,
    f_send,
    f_recv,
    r_send,
    r_recv,
    own_sem,
):
    d, e = lax.axis_index("dp"), lax.axis_index("expert")
    core, ex, ey = e % 2, e // 2 % 2, e // 4
    to_core, to_x, to_y = e + 1 - 2 * core, e + 2 - 4 * ex, e + 4 - 8 * ey
    last = groups - 1
    width = x_v.shape[1]
    piece = 2 * width // 8
    units = gate_v.shape[1]
    count = parts.shape[1]
    over_units = (((1,), (1,)), ((), ()))
    half = pl.ds(core * 4, 4)
    rest = pl.ds(4 - core * 4, 4)

    get_x = pltpu.make_async_copy(x_hbm, x_v, load_sem.at[0])
    get_g = pltpu.make_async_copy(g_hbm, g_v, load_sem.at[1])
    get_w = [
        pltpu.make_async_copy(gate_hbm, gate_v, load_sem.at[2]),
        pltpu.make_async_copy(up_hbm, up_v, load_sem.at[3]),
        pltpu.make_async_copy(down_hbm, down_v, load_sem.at[4]),
    ]
    get_routes = [
        pltpu.make_async_copy(place_hbm, place_ref, load_sem.at[5]),
        pltpu.make_async_copy(ids_hbm, ids_ref, load_sem.at[6]),
        pltpu.make_async_copy(probs_hbm, probs_ref, load_sem.at[7]),
    ]
    for copy in (*get_routes, get_x, get_g):
        copy.start()
    barrier = pltpu.get_barrier_semaphore()

    @pl.when(d < last)
    def _():
        pl.semaphore_signal(barrier, inc=1, device_id=(d + 1, e), device_id_type=MESH)

    @pl.when(d > 0)
    def _():
        pl.semaphore_signal(barrier, inc=1, device_id=(d - 1, e), device_id_type=MESH)

    for k in range(1, slots):
        pl.semaphore_signal(
            barrier, inc=1, device_id=(d, lax.rem(e + k, slots)), device_id_type=MESH
        )
    for copy in get_routes:
        copy.wait()
    chosen = pick(place_ref, ids_ref[...], slots)
    table = tables(chosen)
    probs = probs_ref[...].astype(jnp.float32)
    weight = jnp.concatenate(
        [jnp.sum(c * probs, axis=0, keepdims=True) for c in chosen], axis=0
    )
    plain = stack(table).astype(jnp.bfloat16)
    scaled = stack([t * weight for t in table]).astype(jnp.bfloat16)
    turned = swap(8 * slots)
    get_x.wait()
    get_g.wait()
    for copy in get_w:
        copy.start()
    whole = [
        one_hot_dot(plain if j < 4 else scaled, source[:, j % 4 * piece : (j % 4 + 1) * piece])
        for j, source in enumerate([x_v] * 4 + [g_v] * 4)
    ]
    for r in range(CAP):
        gathered = jnp.concatenate([rows[r * 8 : (r + 1) * 8] for rows in whole], axis=0)
        moved = one_hot_dot(turned, gathered.astype(jnp.bfloat16))
        for s in range(slots):
            packed[s, :, r * piece : (r + 1) * piece] = moved[s * 8 : (s + 1) * 8].astype(
                jnp.bfloat16
            )
    pl.semaphore_wait(barrier, slots - 1 + (d > 0).astype(jnp.int32) + (d < last).astype(jnp.int32))

    def across(j):
        peer = lax.rem(e + j, slots)
        return pltpu.make_async_remote_copy(
            src_ref=packed.at[peer],
            dst_ref=landed.at[d, e],
            send_sem=a_send.at[j - 1],
            recv_sem=a_recv.at[e],
            device_id=(d, peer),
            device_id_type=MESH,
        )

    def arrival(b):
        return pltpu.make_async_remote_copy(
            src_ref=packed.at[b],
            dst_ref=landed.at[d, b],
            send_sem=a_send.at[0],
            recv_sem=a_recv.at[b],
            device_id=(d, b),
            device_id_type=MESH,
        )

    def along(plane, q, way):
        part = landed.at[plane, pl.ds(2 * q, 2)]
        return pltpu.make_async_remote_copy(
            src_ref=part,
            dst_ref=part,
            send_sem=z_send.at[way, plane, q],
            recv_sem=z_recv.at[plane, q],
            device_id=(d + 1 - 2 * way, e),
            device_id_type=MESH,
        )

    for j in range(1, slots):
        across(j).start()
    landed[d, e] = packed[e]
    middle = (d > 0).astype(jnp.int32) * (d < last).astype(jnp.int32)
    inward = d // 2
    outward = 1 - inward
    sign = 1 - 2 * inward
    order = [(ey + i // 2) % 2 * 2 + (ex + i % 2) % 2 for i in range(4)]
    for i, q in enumerate(order):
        for b in (2 * q, 2 * q + 1):

            @pl.when(b != e)
            def _(b=b):
                arrival(b).wait_recv()

        @pl.when((middle == 0) | (i < 2))
        def _(q=q):
            along(d, q, inward).start()

        @pl.when((middle == 1) & (i < 2))
        def _(q=q):
            along(d, q, outward).start()

    has, other = twin_of(place_ref, slots, e)
    core_has, core_other = twin_of(place_ref, slots, to_core)
    mine_out = has & (other // 2 != e // 2)
    core_out = core_has & (core_other // 2 != e // 2)
    target = jnp.where(mine_out, other, core_other) // 2
    from_x = target == to_x // 2

    def choose(first, a, b):
        keep = jnp.full(a.shape, first.astype(jnp.int32)) == 1
        return jnp.where(keep, a.astype(jnp.float32), b.astype(jnp.float32)).astype(jnp.bfloat16)

    def link(source, target_ref, sems, plane, device):
        return pltpu.make_async_remote_copy(
            src_ref=source,
            dst_ref=target_ref,
            send_sem=sems[0].at[plane],
            recv_sem=sems[1].at[plane],
            device_id=(d, device),
            device_id_type=MESH,
        )

    def core_copy(plane):
        return link(landed.at[plane], partner.at[plane], (c_send, c_recv), plane, to_core)

    def x_copy(plane):
        return link(export.at[plane], xin.at[plane], (x_send, x_recv), plane, to_x)

    def y_copy(plane):
        return link(onward.at[plane], yin.at[plane], (y_send, y_recv), plane, to_y)

    def half_copy(plane):
        part = twins.at[plane, half]
        return link(part, part, (t_send, t_recv), plane, to_core)

    def half_arrival(plane):
        part = twins.at[plane, rest]
        return link(part, part, (t_send, t_recv), plane, to_core)

    def relay_x(plane):
        core_copy(plane).wait_recv()
        for b in range(4):
            export[plane, b] = choose(
                mine_out, landed[plane, core * 4 + b], partner[plane, core * 4 + b]
            )
        x_copy(plane).start()

    def relay_y(plane):
        x_copy(plane).wait_recv()
        for b in range(4):
            onward[plane, b] = choose(mine_out | core_out, export[plane, b], xin[plane, b])
        y_copy(plane).start()

    def relay_half(plane):
        y_copy(plane).wait_recv()
        for b in range(4):
            twins[plane, core * 4 + b] = choose(from_x, xin[plane, b], yin[plane, b])
        half_copy(plane).start()

    def unpack(base, block):
        stacked = jnp.concatenate(
            [block(b).astype(jnp.float32) for b in range(8)], axis=0
        ).astype(jnp.bfloat16)
        moved = [
            one_hot_dot(turned, stacked[:, r * piece : (r + 1) * piece]) for r in range(CAP)
        ]
        for j in range(8):
            rows = stack([m[j * 8 : (j + 1) * 8] for m in moved]).astype(jnp.bfloat16)
            if j < 4:
                xs_ref[pl.ds(base, 32), j * piece : (j + 1) * piece] = rows
            else:
                gs_ref[pl.ds(base, 32), (j - 4) * piece : (j - 3) * piece] = rows

    def hidden_grads(base, count):
        rows_x = xs_ref[pl.ds(base, count), :]
        rows_g = gs_ref[pl.ds(base, count), :]
        pre_gate = jnp.dot(rows_x, gate_v[...], preferred_element_type=jnp.float32)
        pre_up = jnp.dot(rows_x, up_v[...], preferred_element_type=jnp.float32)
        back = lax.dot_general(
            rows_g, down_v[...], over_units, preferred_element_type=jnp.float32
        )
        sigma = jax.nn.sigmoid(pre_gate)
        active = pre_gate * sigma
        hidden = active * pre_up
        d_up = (back * active).astype(jnp.bfloat16)
        d_gate = (back * pre_up * sigma * (1.0 + pre_gate * (1.0 - sigma))).astype(jnp.bfloat16)
        du_ref[pl.ds(base, count), :units] = d_gate
        du_ref[pl.ds(base, count), units:] = d_up
        sc_ref[pl.ds(base, count), :] = hidden.astype(jnp.bfloat16)
        return d_gate, d_up, jnp.sum(hidden * back, axis=1, keepdims=True)

    def own_rows(plane):
        base = pl.multiple_of(plane * 32, 32)
        unpack(base, lambda b: landed[plane, b])
        d_gate, d_up, part_dw = hidden_grads(base, 32)
        part = lax.dot_general(
            d_gate, gate_v[...], over_units, preferred_element_type=jnp.float32
        ) + lax.dot_general(d_up, up_v[...], over_units, preferred_element_type=jnp.float32)
        part_dw = jnp.broadcast_to(part_dw, (32, LANES))
        for c in range(count):
            column = part[:, c * LANES : (c + 1) * LANES] if c < count - 1 else part_dw
            for r in range(CAP):
                parts[plane, c, r] = column[r * 8 : (r + 1) * 8].astype(jnp.bfloat16)

    def twin_rows(plane):
        base = pl.multiple_of(groups * 32 + plane * 32, 32)

        def block(b):
            near = partner[plane, b].astype(jnp.float32)
            far = twins[plane, b].astype(jnp.float32)
            take_far = jnp.full(near.shape, mine_out.astype(jnp.int32)) == 1
            take_any = jnp.full(near.shape, has.astype(jnp.int32)) == 1
            return jnp.where(take_any, jnp.where(take_far, far, near), 0.0)

        unpack(base, block)

    cuts = [count * l // LINES for l in range(LINES + 1)]
    cuts = [pl.ds(a, b - a) for a, b in zip(cuts[:-1], cuts[1:])]

    def home(way, plane, l):
        return pltpu.make_async_remote_copy(
            src_ref=parts.at[plane, cuts[l]],
            dst_ref=agg.at[way, plane, cuts[l]],
            send_sem=f_send.at[plane, l],
            recv_sem=f_recv.at[way, plane, l],
            device_id=(d + 1 - 2 * way, e),
            device_id_type=MESH,
        )

    def pass_on(way, plane, l):
        home(way, plane, l).wait_recv()
        both = parts[plane, cuts[l]].astype(jnp.float32) + agg[way, plane, cuts[l]].astype(
            jnp.float32
        )
        parts[plane, cuts[l]] = both.astype(jnp.bfloat16)
        home(way, plane, l).start()

    def finish():
        total[...] = parts[d].astype(jnp.float32)
        for way in range(2):

            @pl.when(d > 0 if way == 0 else d < last)
            def _(way=way):
                for l in range(LINES):
                    home(way, d, l).wait_recv()
                total[...] = total[...] + agg[way, d].astype(jnp.float32)

        columns = []
        for k in range(ret.shape[2] // LANES):
            tall = []
            for j in range(8):
                r, c = divmod(8 * k + j, count)
                tall.append(
                    total[c, r]
                    if r < CAP
                    else jnp.zeros((8, LANES), jnp.float32)
                )
            columns.append(jnp.concatenate(tall, axis=0))
        moved = one_hot_dot(turned, jnp.concatenate(columns, axis=1).astype(jnp.bfloat16))
        for s in range(slots):
            ret[s] = moved[s * 8 : (s + 1) * 8].astype(jnp.bfloat16)
        for j in range(1, slots):
            back_copy(j).start()
        kept().start()

    def back_copy(j):
        peer = lax.rem(e + j, slots)
        return pltpu.make_async_remote_copy(
            src_ref=ret.at[peer],
            dst_ref=back_ref.at[e],
            send_sem=r_send.at[j - 1],
            recv_sem=r_recv.at[j - 1],
            device_id=(d, peer),
            device_id_type=MESH,
        )

    def kept():
        return pltpu.make_async_copy(ret.at[e], back_ref.at[e], own_sem)

    beside, far, near = d - sign, d + 2 * sign, d + sign

    def nth(n):
        return d + sign * ((4 - n) % 4 - 4 * middle * ((n + 3) // 4 - (n + 2) // 4))

    def forward(plane, q, way):
        along(plane, q, way).wait_recv()
        along(plane, q, way).start()

    def middle_first():
        for i in range(4):
            forward(beside, order[i], inward)
            forward(near if i < 2 else far, order[i % 2], outward)
        for q in order[2:]:
            along(d, q, inward).start()
        along(d, order[2], outward).start()

    def middle_second():
        for q in order[2:]:
            forward(far, q, outward)
        along(d, order[3], outward).start()

    def middle_third():
        for q in order[2:]:
            forward(near, q, outward)

    for copy in get_w:
        copy.wait()

    @pl.loop(0, groups + 3)
    def _(n):
        for step, arrive in enumerate((middle_first, middle_second, middle_third)):

            @pl.when((middle == 1) & (n == step + 1))
            def _(arrive=arrive):
                arrive()

        @pl.when(n < groups)
        def _():
            plane = nth(n)

            @pl.when((middle == 0) & (n > 0))
            def _():
                for q in order:
                    along(plane, q, inward).wait_recv()

            core_copy(plane).start()
            own_rows(plane)

            @pl.when((middle == 0) & (n > 0))
            def _():
                for l in range(LINES):
                    home(inward, plane, l).start()

            relay_x(plane)

        @pl.when((n > 0) & (n <= groups))
        def _():
            relay_y(nth(n - 1))

        @pl.when((n == groups) & (middle == 1))
        def _():
            for l in range(LINES):
                pass_on(inward, far, l)
            for l in range(LINES):
                pass_on(outward, beside, l)

        @pl.when(n == groups + 1)
        def _():
            @pl.when(middle == 1)
            def _():
                for l in range(LINES):
                    pass_on(inward, near, l)

            finish()

        @pl.when((n > 1) & (n <= groups + 1))
        def _():
            relay_half(nth(n - 2))

        @pl.when(n > 2)
        def _():
            plane = nth(n - 3)
            half_arrival(plane).wait_recv()
            twin_rows(plane)

    hidden_grads(groups * 32, groups * 32)

    for j in range(1, slots):
        across(j).wait_send()
        back_copy(j).wait()
    kept().wait()
    for plane in range(groups):
        for q in range(4):

            @pl.when((plane <= d) & (d < last))
            def _(plane=plane, q=q):
                along(plane, q, 0).wait_send()

            @pl.when((plane >= d) & (d > 0))
            def _(plane=plane, q=q):
                along(plane, q, 1).wait_send()

        core_copy(plane).wait_send()
        x_copy(plane).wait_send()
        y_copy(plane).wait_send()
        half_copy(plane).wait_send()
        for l in range(LINES):
            for way in range(2):

                @pl.when(plane > d if way == 0 else plane < d)
                def _(plane=plane, way=way, l=l):
                    home(way, plane, l).wait_send()


def exchange(ids, probs, placement, x, g, gate, up, down, groups, slots):
    tokens, width = x.shape
    units = gate.shape[1]
    piece = width // 4
    full = width + LANES
    back = pl.cdiv(CAP * full, 8 * LANES) * LANES
    rows = 2 * groups * 32
    bf16 = jnp.bfloat16
    shape = functools.partial(jax.ShapeDtypeStruct, dtype=bf16)
    vmem, hbm = pl.BlockSpec(memory_space=pltpu.VMEM), pl.BlockSpec(memory_space=pltpu.HBM)
    dma = pltpu.SemaphoreType.DMA
    planes = (groups, 8, 8, CAP * piece)
    halves = (groups, 4, 8, CAP * piece)
    return pl.pallas_call(
        functools.partial(exchange_kernel, groups, slots),
        out_shape=(
            shape((rows, width)),
            shape((rows, width)),
            shape((rows, 2 * units)),
            shape((rows, units)),
            shape((slots, 8, back)),
        ),
        in_specs=[hbm] * 8,
        out_specs=(vmem, vmem, vmem, vmem, pl.BlockSpec(memory_space=pl.ANY)),
        scratch_shapes=[
            pltpu.SMEM(placement.shape, jnp.int32),
            pltpu.VMEM(ids.shape, jnp.int32),
            pltpu.VMEM(probs.shape, bf16),
            pltpu.VMEM((tokens, width), bf16),
            pltpu.VMEM((tokens, width), bf16),
            pltpu.VMEM((width, units), bf16),
            pltpu.VMEM((width, units), bf16),
            pltpu.VMEM((units, width), bf16),
            pltpu.VMEM((slots, 8, CAP * piece), bf16),
            pltpu.VMEM(planes, bf16),
            pltpu.VMEM(planes, bf16),
            pltpu.VMEM(halves, bf16),
            pltpu.VMEM(halves, bf16),
            pltpu.VMEM(halves, bf16),
            pltpu.VMEM(halves, bf16),
            pltpu.VMEM(planes, bf16),
            pltpu.VMEM((groups, full // LANES, CAP, 8, LANES), bf16),
            pltpu.VMEM((2, groups, full // LANES, CAP, 8, LANES), bf16),
            pltpu.VMEM((full // LANES, CAP, 8, LANES), jnp.float32),
            pltpu.VMEM((slots, 8, back), bf16),
            dma((8,)),
            dma((slots - 1,)),
            dma((slots,)),
            dma((2, groups, 4)),
            dma((groups, 4)),
            dma((groups,)),
            dma((groups,)),
            dma((groups,)),
            dma((groups,)),
            dma((groups,)),
            dma((groups,)),
            dma((groups,)),
            dma((groups,)),
            dma((groups, LINES)),
            dma((2, groups, LINES)),
            dma((slots - 1,)),
            dma((slots - 1,)),
            dma,
        ],
        compiler_params=pltpu.CompilerParams(
            collective_id=2, has_side_effects=True, vmem_limit_bytes=36 * 2**20
        ),
    )(
        *(
            pltpu.with_memory_space_constraint(value, pltpu.HBM)
            for value in (placement, ids, probs, x, g, gate, up, down)
        )
    )


def gradient_kernel(
    slots,
    place_ref,
    ids_ref,
    probs_ref,
    xs_ref,
    gs_ref,
    du_ref,
    sc_ref,
    back_ref,
    gg_hbm,
    gu_hbm,
    gd_hbm,
    tokens_hbm,
    route_ref,
    gg_v,
    gu_v,
    gd_v,
    tokens_v,
    rows_v,
    sems,
):
    width = xs_ref.shape[1]
    units = sc_ref.shape[1]
    steps = 7
    step = width // steps
    over_rows = (((0,), (0,)), ((), ()))
    copies = []
    for c in range(steps):
        lanes = pl.ds(c * step, step)
        both = lax.dot_general(
            xs_ref[:, lanes], du_ref[...], over_rows, preferred_element_type=jnp.float32
        )
        gg_v[lanes, :] = both[:, :units].astype(jnp.bfloat16)
        gu_v[lanes, :] = both[:, units:].astype(jnp.bfloat16)
        gd_v[:, lanes] = lax.dot_general(
            sc_ref[...], gs_ref[:, lanes], over_rows, preferred_element_type=jnp.float32
        ).astype(jnp.bfloat16)
        for i, (source, target) in enumerate(
            [
                (gg_v.at[lanes, :], gg_hbm.at[lanes, :]),
                (gu_v.at[lanes, :], gu_hbm.at[lanes, :]),
                (gd_v.at[:, lanes], gd_hbm.at[:, lanes]),
            ]
        ):
            copy = pltpu.make_async_copy(source, target, sems.at[c, i])
            copy.start()
            copies.append(copy)

    chosen = pick(place_ref, ids_ref[...], slots)
    table = tables(chosen)
    stacked = jnp.concatenate(
        [back_ref[s].astype(jnp.float32) for s in range(slots)], axis=0
    ).astype(jnp.bfloat16)
    moved = one_hot_dot(swap(8 * slots), stacked)
    count = rows_v.shape[1] // LANES

    def tile(r, c):
        k, j = divmod(r * count + c, 8)
        return moved[j * 8 : (j + 1) * 8, k * LANES : (k + 1) * LANES]

    for c in range(count - 1):
        rows_v[:, c * LANES : (c + 1) * LANES] = stack(
            [tile(r, c) for r in range(CAP)]
        ).astype(jnp.bfloat16)
    tokens_v[...] = lax.dot_general(
        stack(table).astype(jnp.bfloat16),
        rows_v[:, :width],
        over_rows,
        preferred_element_type=jnp.float32,
    ).astype(jnp.bfloat16)
    copy = pltpu.make_async_copy(tokens_v, tokens_hbm, sems.at[0, 3])
    copy.start()
    copies.append(copy)
    slot_dw = sum(table[r] * tile(r, count - 1) for r in range(CAP))
    route = sum(chosen[s] * slot_dw[s : s + 1] for s in range(slots))
    route_ref[...] = (route / probs_ref[...].astype(jnp.float32)).astype(jnp.bfloat16)
    for copy in copies:
        copy.wait()


def gradients(placement, ids, probs, arrived, slots, tokens):
    xs, gs, du, sc, back = arrived
    width, units = xs.shape[1], sc.shape[1]
    bf16 = jnp.bfloat16
    shape = functools.partial(jax.ShapeDtypeStruct, dtype=bf16)
    vmem, hbm = pl.BlockSpec(memory_space=pltpu.VMEM), pl.BlockSpec(memory_space=pl.ANY)
    return pl.pallas_call(
        functools.partial(gradient_kernel, slots),
        out_shape=(
            shape((width, units)),
            shape((width, units)),
            shape((units, width)),
            shape((tokens, width)),
            shape(probs.shape),
        ),
        in_specs=[pl.BlockSpec(memory_space=pltpu.SMEM)] + [vmem] * 7,
        out_specs=(hbm, hbm, hbm, hbm, vmem),
        scratch_shapes=[
            pltpu.VMEM((width, units), bf16),
            pltpu.VMEM((width, units), bf16),
            pltpu.VMEM((units, width), bf16),
            pltpu.VMEM((tokens, width), bf16),
            pltpu.VMEM((32, width + LANES), bf16),
            pltpu.SemaphoreType.DMA((7, 4)),
        ],
        compiler_params=pltpu.CompilerParams(vmem_limit_bytes=36 * 2**20),
    )(placement, ids, probs, xs, gs, du, sc, back)


def on_small_slice(
    layer_input, output_grad, expert_ids, gate_probs, placement, gate_weight, up_weight, down_weight
):
    slots = lax.axis_size("expert")
    groups = lax.axis_size("dp")
    ids, probs = expert_ids.T, gate_probs.T
    arrived = exchange(
        ids,
        probs,
        placement,
        layer_input,
        output_grad,
        gate_weight[0],
        up_weight[0],
        down_weight[0],
        groups,
        slots,
    )
    grad_gate, grad_up, grad_down, grad_tokens, grad_route = gradients(
        placement, ids, probs, arrived, slots, layer_input.shape[0]
    )
    return grad_tokens, grad_route.T, grad_gate[None], grad_up[None], grad_down[None]


def solution(mesh):
    in_specs = (
        P(("dp", "expert"), None),
        P(("dp", "expert"), None),
        P(("dp", "expert"), None),
        P(("dp", "expert"), None),
        P(),
        P("expert", None, "dp"),
        P("expert", None, "dp"),
        P("expert", "dp", None),
    )
    out_specs = (
        P(("dp", "expert"), None),
        P(("dp", "expert"), None),
        P("expert", None, "dp"),
        P("expert", None, "dp"),
        P("expert", "dp", None),
    )
    small = mesh.shape["dp"] == 4 and mesh.shape["expert"] == 8
    return jax.shard_map(
        on_small_slice if small else on_device, mesh=mesh, in_specs=in_specs, out_specs=out_specs, check_vma=False
    )
```

```python
import functools
import math

import jax
import jax.numpy as jnp
from jax import lax
from jax.experimental import pallas as pl
from jax.experimental.pallas import tpu as pltpu
from jax.sharding import PartitionSpec as P

MESH = pl.DeviceIdType.MESH

CAP = 3
ROWS = 8
LANES = 128
CHUNKS = 4
TILE = 256
LINES = 4


def routes(expert_ids, gate_probs, placement):
    tokens = expert_ids.shape[0]
    slots = placement.shape[0]
    ids = expert_ids.T
    probs = gate_probs.T.astype(jnp.float32)
    topk = ids.shape[0]
    same = placement[:, None] == placement[None, :]
    slot = jnp.arange(slots, dtype=jnp.int32)
    copies = jnp.sum(same.astype(jnp.int32), axis=1)
    rank = jnp.sum((same & (slot[None, :] < slot[:, None])).astype(jnp.int32), axis=1)
    turn = jnp.arange(tokens, dtype=jnp.int32)[None, :] + jnp.arange(topk, dtype=jnp.int32)[:, None]
    chosen = (ids[None] == placement[:, None, None]) & (
        turn[None] % copies[:, None, None] == rank[:, None, None]
    )
    chosen = chosen.astype(jnp.float32)
    hit = jnp.sum(chosen, axis=1)
    weight = jnp.sum(chosen * probs[None], axis=1)
    token = jnp.arange(tokens, dtype=jnp.int32)
    before = (token[:, None] < token[None, :]).astype(jnp.bfloat16)
    position = jnp.dot(hit.astype(jnp.bfloat16), before, preferred_element_type=jnp.float32)
    place = jnp.arange(CAP, dtype=jnp.float32)
    table = hit[:, None, :] * (position[:, None, :] == place[None, :, None]).astype(jnp.float32)
    row_w = jnp.sum(table * weight[:, None, :], axis=-1)
    return chosen, table, row_w, same & (slot[:, None] != slot[None, :])


def meet(groups, slots):
    d, e = lax.axis_index("dp"), lax.axis_index("expert")
    barrier = pltpu.get_barrier_semaphore()
    for k in range(1, groups):
        pl.semaphore_signal(
            barrier, inc=1, device_id=(lax.rem(d + k, groups), e), device_id_type=MESH
        )
    for k in range(1, slots):
        pl.semaphore_signal(
            barrier, inc=1, device_id=(d, lax.rem(e + k, slots)), device_id_type=MESH
        )
    pl.semaphore_wait(barrier, groups + slots - 2)


def spread_kernel(
    groups, slots, u_ref, e_ref, out_ref, landed, ready, z_send, z_recv, p_send, p_recv, own_sem
):
    d, e = lax.axis_index("dp"), lax.axis_index("expert")
    height = u_ref.shape[0]
    third = e_ref.shape[0]
    tail = ready.shape[3] - LANES
    chunk = tail // third
    meet(groups, slots)

    def onward(plane, source, way):
        return pltpu.make_async_remote_copy(
            src_ref=source,
            dst_ref=landed.at[plane],
            send_sem=z_send.at[way, plane],
            recv_sem=z_recv.at[plane],
            device_id=(d + 1 - 2 * way, e),
            device_id_type=MESH,
        )

    def across(plane, j):
        peer = lax.rem(e + j, slots)
        return pltpu.make_async_remote_copy(
            src_ref=ready.at[plane, peer],
            dst_ref=out_ref.at[plane * slots + e],
            send_sem=p_send.at[plane, j - 1],
            recv_sem=p_recv.at[plane, j - 1],
            device_id=(d, peer),
            device_id_type=MESH,
        )

    def stay(plane):
        return pltpu.make_async_copy(
            ready.at[plane, e], out_ref.at[plane * slots + e], own_sem.at[plane]
        )

    def share(plane, read):
        last = read(pl.ds(tail, chunk))
        for c in range(third):
            lanes = pl.ds(c * chunk, chunk)
            rows = jnp.dot(
                e_ref[c, :, :height], read(lanes), preferred_element_type=jnp.float32
            ) + jnp.dot(e_ref[c, :, height:], last, preferred_element_type=jnp.float32)
            for s in range(slots):
                ready[plane, s, :, lanes] = rows[s * ROWS : (s + 1) * ROWS].astype(jnp.bfloat16)
        rows = jnp.dot(
            e_ref[0, :, :height],
            read(pl.ds(tail + chunk, LANES)),
            preferred_element_type=jnp.float32,
        )
        for s in range(slots):
            ready[plane, s, :, pl.ds(tail, LANES)] = rows[s * ROWS : (s + 1) * ROWS].astype(
                jnp.bfloat16
            )
        for j in range(1, slots):
            across(plane, j).start()
        stay(plane).start()

    @pl.when(d + 1 < groups)
    def _():
        onward(d, u_ref, 0).start()

    @pl.when(d > 0)
    def _():
        onward(d, u_ref, 1).start()

    share(d, lambda lanes: u_ref[:, lanes])
    for hop in range(1, groups):
        for way in range(2):
            plane = d - hop if way == 0 else d + hop
            more = d + 1 < groups if way == 0 else d > 0
            here = plane >= 0 if way == 0 else plane < groups

            @pl.when(here)
            def _(plane=plane, more=more, way=way):
                onward(plane, landed.at[plane], way).wait_recv()

                @pl.when(more)
                def _():
                    onward(plane, landed.at[plane], way).start()

                share(plane, lambda lanes: landed[plane, :, lanes])

    for plane in range(groups):

        @pl.when((plane <= d) & (d + 1 < groups))
        def _():
            onward(plane, landed.at[plane], 0).wait_send()

        @pl.when((plane >= d) & (d > 0))
        def _():
            onward(plane, landed.at[plane], 1).wait_send()

        for j in range(1, slots):
            across(plane, j).wait()
        stay(plane).wait()


def dispatch(unique, expand, groups, slots):
    height, width = unique.shape
    packed = 3 * (width - LANES) // 4 + LANES
    landed = (groups, height, width)
    ready = (groups, slots, ROWS, packed)
    need = 2 * (math.prod(landed) + math.prod(ready) + 2 * height * width)
    return pl.pallas_call(
        functools.partial(spread_kernel, groups, slots),
        out_shape=jax.ShapeDtypeStruct((groups * slots, ROWS, packed), jnp.bfloat16),
        in_specs=[pl.BlockSpec(memory_space=pltpu.VMEM)] * 2,
        out_specs=pl.BlockSpec(memory_space=pl.ANY),
        scratch_shapes=[
            pltpu.VMEM(landed, jnp.bfloat16),
            pltpu.VMEM(ready, jnp.bfloat16),
            pltpu.SemaphoreType.DMA((2, groups)),
            pltpu.SemaphoreType.DMA((groups,)),
            pltpu.SemaphoreType.DMA((groups, slots - 1)),
            pltpu.SemaphoreType.DMA((groups, slots - 1)),
            pltpu.SemaphoreType.DMA((groups,)),
        ],
        compiler_params=pltpu.CompilerParams(
            collective_id=0, has_side_effects=True, vmem_limit_bytes=need + 8 * 2**20
        ),
    )(unique, expand)


def arrival_order(groups):
    return sorted(range(1, groups), key=lambda k: (-min(k, groups - k), k))


def fold_kernel(
    groups, slots, p_ref, e_ref, out_ref, landed, sums, z_send, z_recv, p_send, p_recv, own_sem
):
    d, e = lax.axis_index("dp"), lax.axis_index("expert")
    width = p_ref.shape[2]
    step = (width // LANES // CHUNKS) * LANES
    cuts = [pl.ds(c * step, step if c < CHUNKS - 1 else width - c * step) for c in range(CHUNKS)]
    meet(groups, slots)
    along, moved = [], []
    for c, lanes in enumerate(cuts):
        for k in arrival_order(groups):
            plane = lax.rem(d + k, groups)
            copy = pltpu.make_async_remote_copy(
                src_ref=p_ref.at[plane, :, lanes],
                dst_ref=landed.at[k - 1, :, lanes],
                send_sem=z_send.at[c, k - 1],
                recv_sem=z_recv.at[c, k - 1],
                device_id=(plane, e),
                device_id_type=MESH,
            )
            copy.start()
            along.append((c, copy))
    for c, lanes in enumerate(cuts):
        for owner, copy in along:
            if owner == c:
                copy.wait_recv()
        total = p_ref[d, :, lanes].astype(jnp.float32)
        for k in range(1, groups):
            total = total + landed[k - 1, :, lanes].astype(jnp.float32)
        rows = jnp.dot(e_ref[...], total.astype(jnp.bfloat16), preferred_element_type=jnp.float32)
        for s in range(slots):
            sums[s, :, lanes] = rows[s * ROWS : (s + 1) * ROWS].astype(jnp.bfloat16)
        for j in range(1, slots):
            peer = lax.rem(e + j, slots)
            copy = pltpu.make_async_remote_copy(
                src_ref=sums.at[peer, :, lanes],
                dst_ref=out_ref.at[e, :, lanes],
                send_sem=p_send.at[c, j - 1],
                recv_sem=p_recv.at[c, j - 1],
                device_id=(d, peer),
                device_id_type=MESH,
            )
            copy.start()
            moved.append(copy)
    kept = pltpu.make_async_copy(sums.at[e], out_ref.at[e], own_sem)
    kept.start()
    for _, copy in along:
        copy.wait_send()
    for copy in moved:
        copy.wait()
    kept.wait()


def combine(partial, expand, groups, slots):
    _, height, width = partial.shape
    need = 2 * (2 * groups * height * width + slots * ROWS * width)
    return pl.pallas_call(
        functools.partial(fold_kernel, groups, slots),
        out_shape=jax.ShapeDtypeStruct((slots, ROWS, width), jnp.bfloat16),
        in_specs=[pl.BlockSpec(memory_space=pltpu.VMEM)] * 2,
        out_specs=pl.BlockSpec(memory_space=pl.ANY),
        scratch_shapes=[
            pltpu.VMEM((groups - 1, height, width), jnp.bfloat16),
            pltpu.VMEM((slots, ROWS, width), jnp.bfloat16),
            pltpu.SemaphoreType.DMA((CHUNKS, groups - 1)),
            pltpu.SemaphoreType.DMA((CHUNKS, groups - 1)),
            pltpu.SemaphoreType.DMA((CHUNKS, slots - 1)),
            pltpu.SemaphoreType.DMA((CHUNKS, slots - 1)),
            pltpu.SemaphoreType.DMA,
        ],
        compiler_params=pltpu.CompilerParams(
            collective_id=1, has_side_effects=True, vmem_limit_bytes=need + 8 * 2**20
        ),
    )(partial, expand)


def expert_kernel(
    a_ref, gate_ref, up_ref, down_ref, gg_ref, gu_ref, gd_ref, part_ref, g_ref, du_ref, sc_ref
):
    count = a_ref.shape[0]
    width, units = gate_ref.shape
    packed = a_ref.shape[1] - LANES
    rest = packed // CAP
    own_rows = TILE // ROWS * CAP
    over_units = (((1,), (1,)), ((), ()))
    over_rows = (((0,), (0,)), ((), ()))

    @pl.loop(0, count // TILE)
    def _(t):
        here = pl.ds(pl.multiple_of(t * TILE, TILE), TILE)
        row = lax.broadcasted_iota(jnp.int32, (TILE, TILE), 0)
        col = lax.broadcasted_iota(jnp.int32, (TILE, TILE), 1)
        place = row % ROWS
        source = row - place + 2 * CAP + (place >= CAP).astype(jnp.int32)
        tail = jnp.zeros((TILE, rest), jnp.float32)
        for c in range(CAP):
            pick = (col == source) & (place < 2 * CAP) & (place % CAP == c)
            tail = tail + jnp.dot(
                pick.astype(jnp.float32).astype(jnp.bfloat16),
                a_ref[here, c * rest : (c + 1) * rest],
                preferred_element_type=jnp.float32,
            )
        g_ref[here, : packed - width] = a_ref[here, width:packed]
        g_ref[here, packed - width :] = tail.astype(jnp.bfloat16)
        flat_x = a_ref[here, :width]
        scale = a_ref[here, packed : packed + LANES].astype(jnp.float32)[:, :1]
        pre_gate = jnp.dot(flat_x, gate_ref[...], preferred_element_type=jnp.float32)
        pre_up = jnp.dot(flat_x, up_ref[...], preferred_element_type=jnp.float32)
        back = lax.dot_general(
            g_ref[here, :], down_ref[...], over_units, preferred_element_type=jnp.float32
        )
        sigma = jax.nn.sigmoid(pre_gate)
        active = pre_gate * sigma
        hidden = active * pre_up
        d_hidden = scale * back
        unit_row = lax.broadcasted_iota(jnp.int32, (TILE, units), 0)
        real = unit_row % ROWS < 2 * CAP

        def masked(values):
            return jnp.where(real, values, 0.0)

        d_up = masked(d_hidden * active).astype(jnp.bfloat16)
        d_gate = masked(d_hidden * pre_up * sigma * (1.0 + pre_gate * (1.0 - sigma))).astype(
            jnp.bfloat16
        )
        du_ref[here, :units] = d_gate
        du_ref[here, units:] = d_up
        sc_ref[here, :] = masked(scale * hidden).astype(jnp.bfloat16)
        part_dw = jnp.sum(masked(hidden * back), axis=1, keepdims=True)
        part_dw = jnp.broadcast_to(part_dw, (TILE, LANES)).astype(jnp.bfloat16)
        target = lax.broadcasted_iota(jnp.int32, (own_rows, TILE), 0)
        origin = lax.broadcasted_iota(jnp.int32, (own_rows, TILE), 1)
        keep = (origin == target // CAP * ROWS + target % CAP).astype(jnp.float32)
        keep = keep.astype(jnp.bfloat16)

        def own(values):
            return jnp.dot(keep, values, preferred_element_type=jnp.float32).astype(jnp.bfloat16)

        own_gate, own_up = own(d_gate), own(d_up)
        out = pl.ds(pl.multiple_of(t * own_rows, 8), own_rows)
        part = lax.dot_general(
            own_gate, gate_ref[...], over_units, preferred_element_type=jnp.float32
        ) + lax.dot_general(own_up, up_ref[...], over_units, preferred_element_type=jnp.float32)
        part_ref[out, :width] = part.astype(jnp.bfloat16)
        part_ref[out, width:] = own(part_dw)

    step = width // 7

    @pl.loop(0, 7)
    def _(c):
        lanes = pl.ds(pl.multiple_of(c * step, LANES), step)
        both = lax.dot_general(
            a_ref[:, lanes], du_ref[...], over_rows, preferred_element_type=jnp.float32
        )
        gg_ref[lanes, :] = both[:, :units].astype(jnp.bfloat16)
        gu_ref[lanes, :] = both[:, units:].astype(jnp.bfloat16)
        down = lax.dot_general(
            sc_ref[...], g_ref[:, lanes], over_rows, preferred_element_type=jnp.float32
        )
        gd_ref[:, lanes] = down.astype(jnp.bfloat16)


def expert_step(arrived, gate_block, up_block, down_block):
    count, packed = arrived.shape
    width, units = gate_block.shape
    part = (count // ROWS * CAP, width + LANES)
    need = 2 * (
        count * (packed + width + 3 * units) + 6 * width * units + part[0] * part[1]
    )
    shape = functools.partial(jax.ShapeDtypeStruct, dtype=jnp.bfloat16)
    return pl.pallas_call(
        expert_kernel,
        out_shape=(
            shape((width, units)),
            shape((width, units)),
            shape((units, width)),
            shape(part),
        ),
        in_specs=[pl.BlockSpec(memory_space=pltpu.VMEM)] * 4,
        out_specs=tuple([pl.BlockSpec(memory_space=pltpu.VMEM)] * 4),
        scratch_shapes=[
            pltpu.VMEM((count, width), jnp.bfloat16),
            pltpu.VMEM((count, 2 * units), jnp.bfloat16),
            pltpu.VMEM((count, units), jnp.bfloat16),
        ],
        compiler_params=pltpu.CompilerParams(
            vmem_limit_bytes=min(need + 16 * 2**20, 63 * 2**20)
        ),
    )(arrived, gate_block, up_block, down_block)


def on_device(
    layer_input, output_grad, expert_ids, gate_probs, placement, gate_weight, up_weight, down_weight
):
    slots = lax.axis_size("expert")
    groups = lax.axis_size("dp")
    tokens, width = layer_input.shape
    blocks = slots * groups
    chosen, table, row_w, twin = routes(expert_ids, gate_probs, placement)
    token_table = table.reshape(slots * CAP, tokens).astype(jnp.bfloat16)
    send_x = jnp.dot(token_table, layer_input, preferred_element_type=jnp.float32)
    send_g = jnp.dot(token_table, output_grad, preferred_element_type=jnp.float32)
    unique = jnp.concatenate(
        [send_x, send_g, jnp.broadcast_to(row_w.reshape(slots * CAP, 1), (slots * CAP, LANES))],
        axis=1,
    ).astype(jnp.bfloat16)

    row = jnp.arange(ROWS, dtype=jnp.int32)
    cap = jnp.arange(CAP, dtype=jnp.int32)
    eye = jnp.eye(slots, dtype=jnp.float32)[:, None, :, None]
    others = twin.astype(jnp.float32)[:, None, :, None]

    def layout(pick_mine, pick_theirs):
        spread = eye * pick_mine[None, :, None, :] + others * pick_theirs[None, :, None, :]
        return spread.reshape(slots * ROWS, slots * CAP)

    mine = (row[:, None] == cap[None, :]).astype(jnp.float32)
    theirs = (row[:, None] == cap[None, :] + CAP).astype(jnp.float32)
    main = layout(mine, theirs)
    expand = jnp.stack(
        [
            jnp.concatenate(
                [
                    main,
                    layout(
                        ((row[:, None] == 2 * CAP) & (cap[None, :] == c)).astype(jnp.float32),
                        ((row[:, None] == 2 * CAP + 1) & (cap[None, :] == c)).astype(jnp.float32),
                    ),
                ],
                axis=1,
            )
            for c in range(CAP)
        ]
    ).astype(jnp.bfloat16)

    arrived = dispatch(unique, expand, groups, slots)
    grad_gate, grad_up, grad_down, partial = expert_step(
        arrived.reshape(blocks * ROWS, arrived.shape[2]),
        gate_weight[0],
        up_weight[0],
        down_weight[0],
    )
    partial = partial.reshape(groups, slots * CAP, width + LANES)
    spread = (eye * mine[None, :, None, :]).reshape(slots * ROWS, slots * CAP).astype(jnp.bfloat16)
    back_rows = combine(partial, spread, groups, slots).reshape(slots * ROWS, width + LANES)

    wide = jnp.einsum("rc,sct->srt", mine, table).reshape(slots * ROWS, tokens).astype(jnp.bfloat16)
    grad_tokens = lax.dot_general(
        wide, back_rows[:, :width], (((0,), (0,)), ((), ())), preferred_element_type=jnp.float32
    ).astype(jnp.bfloat16)
    row_dw = back_rows[:, width].astype(jnp.float32)
    slot_dw = jnp.sum(
        (wide.astype(jnp.float32) * row_dw[:, None]).reshape(slots, ROWS, tokens), axis=1
    )
    grad_route = jnp.sum(chosen * slot_dw[:, None, :], axis=0).T.astype(jnp.bfloat16)
    return (
        grad_tokens,
        grad_route,
        grad_gate[None],
        grad_up[None],
        grad_down[None],
    )


def swap(count):
    row = lax.broadcasted_iota(jnp.int32, (count, count), 0)
    col = lax.broadcasted_iota(jnp.int32, (count, count), 1)
    return (col == row % 8 * 8 + row // 8).astype(jnp.float32).astype(jnp.bfloat16)


def one_hot_dot(table, values):
    return jnp.dot(table, values, preferred_element_type=jnp.float32)


def pick(place_ref, ids, slots):
    held = [place_ref[s] for s in range(slots)]
    turn = lax.broadcasted_iota(jnp.int32, ids.shape, 0) + lax.broadcasted_iota(
        jnp.int32, ids.shape, 1
    )
    chosen = []
    for s in range(slots):
        same = [(held[s] == held[q]).astype(jnp.int32) for q in range(slots)]
        copies, rank = sum(same), sum(same[:s], jnp.int32(0))
        chosen.append(
            ((ids == held[s]) & ((turn & (copies - 1)) == rank)).astype(jnp.float32)
        )
    return chosen


def tables(chosen):
    hit = jnp.concatenate([jnp.sum(c, axis=0, keepdims=True) for c in chosen], axis=0)
    tokens = hit.shape[1]
    row = lax.broadcasted_iota(jnp.int32, (tokens, tokens), 0)
    col = lax.broadcasted_iota(jnp.int32, (tokens, tokens), 1)
    before = (row < col).astype(jnp.float32).astype(jnp.bfloat16)
    position = one_hot_dot(hit.astype(jnp.bfloat16), before)
    return [jnp.where(position == float(r), hit, 0.0) for r in range(CAP)]


def stack(parts):
    return jnp.concatenate([*parts, jnp.zeros_like(parts[0])], axis=0)


def twin_of(place_ref, slots, e):
    mine = jnp.int32(0)
    for s in range(slots):
        mine = jnp.where(e == s, place_ref[s], mine)
    found, other = jnp.int32(0), jnp.int32(0)
    for s in range(slots):
        same = ((place_ref[s] == mine) & (e != s)).astype(jnp.int32)
        found = found + same
        other = other + same * s
    return found > 0, other


def exchange_kernel(
    groups,
    slots,
    place_hbm,
    ids_hbm,
    probs_hbm,
    x_hbm,
    g_hbm,
    gate_hbm,
    up_hbm,
    down_hbm,
    xs_ref,
    gs_ref,
    du_ref,
    sc_ref,
    back_ref,
    place_ref,
    ids_ref,
    probs_ref,
    x_v,
    g_v,
    gate_v,
    up_v,
    down_v,
    packed,
    landed,
    partner,
    export,
    xin,
    onward,
    yin,
    twins,
    parts,
    agg,
    total,
    ret,
    load_sem,
    a_send,
    a_recv,
    z_send,
    z_recv,
    c_send,
    c_recv,
    x_send,
    x_recv,
    y_send,
    y_recv,
    t_send,
    t_recv,
    f_send,
    f_recv,
    r_send,
    r_recv,
    own_sem,
):
    d, e = lax.axis_index("dp"), lax.axis_index("expert")
    core, ex, ey = e % 2, e // 2 % 2, e // 4
    to_core, to_x, to_y = e + 1 - 2 * core, e + 2 - 4 * ex, e + 4 - 8 * ey
    last = groups - 1
    width = x_v.shape[1]
    piece = 2 * width // 8
    units = gate_v.shape[1]
    count = parts.shape[1]
    over_units = (((1,), (1,)), ((), ()))
    half = pl.ds(core * 4, 4)
    rest = pl.ds(4 - core * 4, 4)

    get_x = pltpu.make_async_copy(x_hbm, x_v, load_sem.at[0])
    get_g = pltpu.make_async_copy(g_hbm, g_v, load_sem.at[1])
    get_w = [
        pltpu.make_async_copy(gate_hbm, gate_v, load_sem.at[2]),
        pltpu.make_async_copy(up_hbm, up_v, load_sem.at[3]),
        pltpu.make_async_copy(down_hbm, down_v, load_sem.at[4]),
    ]
    get_routes = [
        pltpu.make_async_copy(place_hbm, place_ref, load_sem.at[5]),
        pltpu.make_async_copy(ids_hbm, ids_ref, load_sem.at[6]),
        pltpu.make_async_copy(probs_hbm, probs_ref, load_sem.at[7]),
    ]
    for copy in (*get_routes, get_x, get_g):
        copy.start()
    barrier = pltpu.get_barrier_semaphore()

    @pl.when(d < last)
    def _():
        pl.semaphore_signal(barrier, inc=1, device_id=(d + 1, e), device_id_type=MESH)

    @pl.when(d > 0)
    def _():
        pl.semaphore_signal(barrier, inc=1, device_id=(d - 1, e), device_id_type=MESH)

    for k in range(1, slots):
        pl.semaphore_signal(
            barrier, inc=1, device_id=(d, lax.rem(e + k, slots)), device_id_type=MESH
        )
    for copy in get_routes:
        copy.wait()
    chosen = pick(place_ref, ids_ref[...], slots)
    table = tables(chosen)
    probs = probs_ref[...].astype(jnp.float32)
    weight = jnp.concatenate(
        [jnp.sum(c * probs, axis=0, keepdims=True) for c in chosen], axis=0
    )
    plain = stack(table).astype(jnp.bfloat16)
    scaled = stack([t * weight for t in table]).astype(jnp.bfloat16)
    turned = swap(8 * slots)
    get_x.wait()
    get_g.wait()
    for copy in get_w:
        copy.start()
    whole = [
        one_hot_dot(plain if j < 4 else scaled, source[:, j % 4 * piece : (j % 4 + 1) * piece])
        for j, source in enumerate([x_v] * 4 + [g_v] * 4)
    ]
    for r in range(CAP):
        gathered = jnp.concatenate([rows[r * 8 : (r + 1) * 8] for rows in whole], axis=0)
        moved = one_hot_dot(turned, gathered.astype(jnp.bfloat16))
        for s in range(slots):
            packed[s, :, r * piece : (r + 1) * piece] = moved[s * 8 : (s + 1) * 8].astype(
                jnp.bfloat16
            )
    pl.semaphore_wait(barrier, slots - 1 + (d > 0).astype(jnp.int32) + (d < last).astype(jnp.int32))

    def across(j):
        peer = lax.rem(e + j, slots)
        return pltpu.make_async_remote_copy(
            src_ref=packed.at[peer],
            dst_ref=landed.at[d, e],
            send_sem=a_send.at[j - 1],
            recv_sem=a_recv.at[e],
            device_id=(d, peer),
            device_id_type=MESH,
        )

    def arrival(b):
        return pltpu.make_async_remote_copy(
            src_ref=packed.at[b],
            dst_ref=landed.at[d, b],
            send_sem=a_send.at[0],
            recv_sem=a_recv.at[b],
            device_id=(d, b),
            device_id_type=MESH,
        )

    def along(plane, q, way):
        part = landed.at[plane, pl.ds(2 * q, 2)]
        return pltpu.make_async_remote_copy(
            src_ref=part,
            dst_ref=part,
            send_sem=z_send.at[way, plane, q],
            recv_sem=z_recv.at[plane, q],
            device_id=(d + 1 - 2 * way, e),
            device_id_type=MESH,
        )

    for j in range(1, slots):
        across(j).start()
    landed[d, e] = packed[e]
    middle = (d > 0).astype(jnp.int32) * (d < last).astype(jnp.int32)
    inward = d // 2
    outward = 1 - inward
    sign = 1 - 2 * inward
    order = [(ey + i // 2) % 2 * 2 + (ex + i % 2) % 2 for i in range(4)]
    for i, q in enumerate(order):
        for b in (2 * q, 2 * q + 1):

            @pl.when(b != e)
            def _(b=b):
                arrival(b).wait_recv()

        @pl.when((middle == 0) | (i < 2))
        def _(q=q):
            along(d, q, inward).start()

        @pl.when((middle == 1) & (i < 2))
        def _(q=q):
            along(d, q, outward).start()

    has, other = twin_of(place_ref, slots, e)
    core_has, core_other = twin_of(place_ref, slots, to_core)
    mine_out = has & (other // 2 != e // 2)
    core_out = core_has & (core_other // 2 != e // 2)
    target = jnp.where(mine_out, other, core_other) // 2
    from_x = target == to_x // 2

    def choose(first, a, b):
        keep = jnp.full(a.shape, first.astype(jnp.int32)) == 1
        return jnp.where(keep, a.astype(jnp.float32), b.astype(jnp.float32)).astype(jnp.bfloat16)

    def link(source, target_ref, sems, plane, device):
        return pltpu.make_async_remote_copy(
            src_ref=source,
            dst_ref=target_ref,
            send_sem=sems[0].at[plane],
            recv_sem=sems[1].at[plane],
            device_id=(d, device),
            device_id_type=MESH,
        )

    def core_copy(plane):
        return link(landed.at[plane], partner.at[plane], (c_send, c_recv), plane, to_core)

    def x_copy(plane):
        return link(export.at[plane], xin.at[plane], (x_send, x_recv), plane, to_x)

    def y_copy(plane):
        return link(onward.at[plane], yin.at[plane], (y_send, y_recv), plane, to_y)

    def half_copy(plane):
        part = twins.at[plane, half]
        return link(part, part, (t_send, t_recv), plane, to_core)

    def half_arrival(plane):
        part = twins.at[plane, rest]
        return link(part, part, (t_send, t_recv), plane, to_core)

    def relay_x(plane):
        core_copy(plane).wait_recv()
        for b in range(4):
            export[plane, b] = choose(
                mine_out, landed[plane, core * 4 + b], partner[plane, core * 4 + b]
            )
        x_copy(plane).start()

    def relay_y(plane):
        x_copy(plane).wait_recv()
        for b in range(4):
            onward[plane, b] = choose(mine_out | core_out, export[plane, b], xin[plane, b])
        y_copy(plane).start()

    def relay_half(plane):
        y_copy(plane).wait_recv()
        for b in range(4):
            twins[plane, core * 4 + b] = choose(from_x, xin[plane, b], yin[plane, b])
        half_copy(plane).start()

    def unpack(base, block):
        stacked = jnp.concatenate(
            [block(b).astype(jnp.float32) for b in range(8)], axis=0
        ).astype(jnp.bfloat16)
        moved = [
            one_hot_dot(turned, stacked[:, r * piece : (r + 1) * piece]) for r in range(CAP)
        ]
        for j in range(8):
            rows = stack([m[j * 8 : (j + 1) * 8] for m in moved]).astype(jnp.bfloat16)
            if j < 4:
                xs_ref[pl.ds(base, 32), j * piece : (j + 1) * piece] = rows
            else:
                gs_ref[pl.ds(base, 32), (j - 4) * piece : (j - 3) * piece] = rows

    def hidden_grads(base, count):
        rows_x = xs_ref[pl.ds(base, count), :]
        rows_g = gs_ref[pl.ds(base, count), :]
        pre_gate = jnp.dot(rows_x, gate_v[...], preferred_element_type=jnp.float32)
        pre_up = jnp.dot(rows_x, up_v[...], preferred_element_type=jnp.float32)
        back = lax.dot_general(
            rows_g, down_v[...], over_units, preferred_element_type=jnp.float32
        )
        sigma = jax.nn.sigmoid(pre_gate)
        active = pre_gate * sigma
        hidden = active * pre_up
        d_up = (back * active).astype(jnp.bfloat16)
        d_gate = (back * pre_up * sigma * (1.0 + pre_gate * (1.0 - sigma))).astype(jnp.bfloat16)
        du_ref[pl.ds(base, count), :units] = d_gate
        du_ref[pl.ds(base, count), units:] = d_up
        sc_ref[pl.ds(base, count), :] = hidden.astype(jnp.bfloat16)
        return d_gate, d_up, jnp.sum(hidden * back, axis=1, keepdims=True)

    def own_rows(plane):
        base = pl.multiple_of(plane * 32, 32)
        unpack(base, lambda b: landed[plane, b])
        d_gate, d_up, part_dw = hidden_grads(base, 32)
        part = lax.dot_general(
            d_gate, gate_v[...], over_units, preferred_element_type=jnp.float32
        ) + lax.dot_general(d_up, up_v[...], over_units, preferred_element_type=jnp.float32)
        part_dw = jnp.broadcast_to(part_dw, (32, LANES))
        for c in range(count):
            column = part[:, c * LANES : (c + 1) * LANES] if c < count - 1 else part_dw
            for r in range(CAP):
                parts[plane, c, r] = column[r * 8 : (r + 1) * 8].astype(jnp.bfloat16)

    def twin_rows(plane):
        base = pl.multiple_of(groups * 32 + plane * 32, 32)

        def block(b):
            near = partner[plane, b].astype(jnp.float32)
            far = twins[plane, b].astype(jnp.float32)
            take_far = jnp.full(near.shape, mine_out.astype(jnp.int32)) == 1
            take_any = jnp.full(near.shape, has.astype(jnp.int32)) == 1
            return jnp.where(take_any, jnp.where(take_far, far, near), 0.0)

        unpack(base, block)

    cuts = [count * l // LINES for l in range(LINES + 1)]
    cuts = [pl.ds(a, b - a) for a, b in zip(cuts[:-1], cuts[1:])]

    def home(way, plane, l):
        return pltpu.make_async_remote_copy(
            src_ref=parts.at[plane, cuts[l]],
            dst_ref=agg.at[way, plane, cuts[l]],
            send_sem=f_send.at[plane, l],
            recv_sem=f_recv.at[way, plane, l],
            device_id=(d + 1 - 2 * way, e),
            device_id_type=MESH,
        )

    def pass_on(way, plane, l):
        home(way, plane, l).wait_recv()
        both = parts[plane, cuts[l]].astype(jnp.float32) + agg[way, plane, cuts[l]].astype(
            jnp.float32
        )
        parts[plane, cuts[l]] = both.astype(jnp.bfloat16)
        home(way, plane, l).start()

    def finish():
        total[...] = parts[d].astype(jnp.float32)
        for way in range(2):

            @pl.when(d > 0 if way == 0 else d < last)
            def _(way=way):
                for l in range(LINES):
                    home(way, d, l).wait_recv()
                total[...] = total[...] + agg[way, d].astype(jnp.float32)

        columns = []
        for k in range(ret.shape[2] // LANES):
            tall = []
            for j in range(8):
                r, c = divmod(8 * k + j, count)
                tall.append(
                    total[c, r]
                    if r < CAP
                    else jnp.zeros((8, LANES), jnp.float32)
                )
            columns.append(jnp.concatenate(tall, axis=0))
        moved = one_hot_dot(turned, jnp.concatenate(columns, axis=1).astype(jnp.bfloat16))
        for s in range(slots):
            ret[s] = moved[s * 8 : (s + 1) * 8].astype(jnp.bfloat16)
        for j in range(1, slots):
            back_copy(j).start()
        kept().start()

    def back_copy(j):
        peer = lax.rem(e + j, slots)
        return pltpu.make_async_remote_copy(
            src_ref=ret.at[peer],
            dst_ref=back_ref.at[e],
            send_sem=r_send.at[j - 1],
            recv_sem=r_recv.at[j - 1],
            device_id=(d, peer),
            device_id_type=MESH,
        )

    def kept():
        return pltpu.make_async_copy(ret.at[e], back_ref.at[e], own_sem)

    beside, far, near = d - sign, d + 2 * sign, d + sign

    def nth(n):
        return d + sign * ((4 - n) % 4 - 4 * middle * ((n + 3) // 4 - (n + 2) // 4))

    def forward(plane, q, way):
        along(plane, q, way).wait_recv()
        along(plane, q, way).start()

    def middle_first():
        for i in range(4):
            forward(beside, order[i], inward)
            forward(near if i < 2 else far, order[i % 2], outward)
        for q in order[2:]:
            along(d, q, inward).start()
        along(d, order[2], outward).start()

    def middle_second():
        for q in order[2:]:
            forward(far, q, outward)
        along(d, order[3], outward).start()

    def middle_third():
        for q in order[2:]:
            forward(near, q, outward)

    for copy in get_w:
        copy.wait()

    @pl.loop(0, groups + 3)
    def _(n):
        for step, arrive in enumerate((middle_first, middle_second, middle_third)):

            @pl.when((middle == 1) & (n == step + 1))
            def _(arrive=arrive):
                arrive()

        @pl.when(n < groups)
        def _():
            plane = nth(n)

            @pl.when((middle == 0) & (n > 0))
            def _():
                for q in order:
                    along(plane, q, inward).wait_recv()

            core_copy(plane).start()

            @pl.when(n == groups - 1)
            def _():
                relay_x(plane)

            own_rows(plane)

            @pl.when((middle == 0) & (n > 0))
            def _():
                for l in range(LINES):
                    home(inward, plane, l).start()

            @pl.when(n < groups - 1)
            def _():
                relay_x(plane)

        @pl.when((n > 0) & (n <= groups))
        def _():
            relay_y(nth(n - 1))

        @pl.when((n == groups) & (middle == 1))
        def _():
            for l in range(LINES):
                pass_on(inward, far, l)
            for l in range(LINES):
                pass_on(outward, beside, l)

        @pl.when(n == groups + 1)
        def _():
            @pl.when(middle == 1)
            def _():
                for l in range(LINES):
                    pass_on(inward, near, l)

            finish()

        @pl.when((n > 1) & (n <= groups + 1))
        def _():
            relay_half(nth(n - 2))

        @pl.when(n > 2)
        def _():
            plane = nth(n - 3)
            half_arrival(plane).wait_recv()
            twin_rows(plane)

    hidden_grads(groups * 32, groups * 32)

    for j in range(1, slots):
        across(j).wait_send()
        back_copy(j).wait()
    kept().wait()
    for plane in range(groups):
        for q in range(4):

            @pl.when((plane <= d) & (d < last))
            def _(plane=plane, q=q):
                along(plane, q, 0).wait_send()

            @pl.when((plane >= d) & (d > 0))
            def _(plane=plane, q=q):
                along(plane, q, 1).wait_send()

        core_copy(plane).wait_send()
        x_copy(plane).wait_send()
        y_copy(plane).wait_send()
        half_copy(plane).wait_send()
        for l in range(LINES):
            for way in range(2):

                @pl.when(plane > d if way == 0 else plane < d)
                def _(plane=plane, way=way, l=l):
                    home(way, plane, l).wait_send()


def exchange(ids, probs, placement, x, g, gate, up, down, groups, slots):
    tokens, width = x.shape
    units = gate.shape[1]
    piece = width // 4
    full = width + LANES
    back = pl.cdiv(CAP * full, 8 * LANES) * LANES
    rows = 2 * groups * 32
    bf16 = jnp.bfloat16
    shape = functools.partial(jax.ShapeDtypeStruct, dtype=bf16)
    vmem, hbm = pl.BlockSpec(memory_space=pltpu.VMEM), pl.BlockSpec(memory_space=pltpu.HBM)
    dma = pltpu.SemaphoreType.DMA
    planes = (groups, 8, 8, CAP * piece)
    halves = (groups, 4, 8, CAP * piece)
    return pl.pallas_call(
        functools.partial(exchange_kernel, groups, slots),
        out_shape=(
            shape((rows, width)),
            shape((rows, width)),
            shape((rows, 2 * units)),
            shape((rows, units)),
            shape((slots, 8, back)),
        ),
        in_specs=[hbm] * 8,
        out_specs=(vmem, vmem, vmem, vmem, pl.BlockSpec(memory_space=pl.ANY)),
        scratch_shapes=[
            pltpu.SMEM(placement.shape, jnp.int32),
            pltpu.VMEM(ids.shape, jnp.int32),
            pltpu.VMEM(probs.shape, bf16),
            pltpu.VMEM((tokens, width), bf16),
            pltpu.VMEM((tokens, width), bf16),
            pltpu.VMEM((width, units), bf16),
            pltpu.VMEM((width, units), bf16),
            pltpu.VMEM((units, width), bf16),
            pltpu.VMEM((slots, 8, CAP * piece), bf16),
            pltpu.VMEM(planes, bf16),
            pltpu.VMEM(planes, bf16),
            pltpu.VMEM(halves, bf16),
            pltpu.VMEM(halves, bf16),
            pltpu.VMEM(halves, bf16),
            pltpu.VMEM(halves, bf16),
            pltpu.VMEM(planes, bf16),
            pltpu.VMEM((groups, full // LANES, CAP, 8, LANES), bf16),
            pltpu.VMEM((2, groups, full // LANES, CAP, 8, LANES), bf16),
            pltpu.VMEM((full // LANES, CAP, 8, LANES), jnp.float32),
            pltpu.VMEM((slots, 8, back), bf16),
            dma((8,)),
            dma((slots - 1,)),
            dma((slots,)),
            dma((2, groups, 4)),
            dma((groups, 4)),
            dma((groups,)),
            dma((groups,)),
            dma((groups,)),
            dma((groups,)),
            dma((groups,)),
            dma((groups,)),
            dma((groups,)),
            dma((groups,)),
            dma((groups, LINES)),
            dma((2, groups, LINES)),
            dma((slots - 1,)),
            dma((slots - 1,)),
            dma,
        ],
        compiler_params=pltpu.CompilerParams(
            collective_id=2, has_side_effects=True, vmem_limit_bytes=36 * 2**20
        ),
    )(
        *(
            pltpu.with_memory_space_constraint(value, pltpu.HBM)
            for value in (placement, ids, probs, x, g, gate, up, down)
        )
    )


def gradient_kernel(
    slots,
    place_ref,
    ids_ref,
    probs_ref,
    xs_ref,
    gs_ref,
    du_ref,
    sc_ref,
    back_ref,
    gg_hbm,
    gu_hbm,
    gd_hbm,
    tokens_hbm,
    route_ref,
    gg_v,
    gu_v,
    gd_v,
    tokens_v,
    rows_v,
    sems,
):
    width = xs_ref.shape[1]
    units = sc_ref.shape[1]
    steps = 7
    step = width // steps
    over_rows = (((0,), (0,)), ((), ()))
    copies = []
    for c in range(steps):
        lanes = pl.ds(c * step, step)
        both = lax.dot_general(
            xs_ref[:, lanes], du_ref[...], over_rows, preferred_element_type=jnp.float32
        )
        gg_v[lanes, :] = both[:, :units].astype(jnp.bfloat16)
        gu_v[lanes, :] = both[:, units:].astype(jnp.bfloat16)
        gd_v[:, lanes] = lax.dot_general(
            sc_ref[...], gs_ref[:, lanes], over_rows, preferred_element_type=jnp.float32
        ).astype(jnp.bfloat16)
        for i, (source, target) in enumerate(
            [
                (gg_v.at[lanes, :], gg_hbm.at[lanes, :]),
                (gu_v.at[lanes, :], gu_hbm.at[lanes, :]),
                (gd_v.at[:, lanes], gd_hbm.at[:, lanes]),
            ]
        ):
            copy = pltpu.make_async_copy(source, target, sems.at[c, i])
            copy.start()
            copies.append(copy)

    chosen = pick(place_ref, ids_ref[...], slots)
    table = tables(chosen)
    stacked = jnp.concatenate(
        [back_ref[s].astype(jnp.float32) for s in range(slots)], axis=0
    ).astype(jnp.bfloat16)
    moved = one_hot_dot(swap(8 * slots), stacked)
    count = rows_v.shape[1] // LANES

    def tile(r, c):
        k, j = divmod(r * count + c, 8)
        return moved[j * 8 : (j + 1) * 8, k * LANES : (k + 1) * LANES]

    for c in range(count - 1):
        rows_v[:, c * LANES : (c + 1) * LANES] = stack(
            [tile(r, c) for r in range(CAP)]
        ).astype(jnp.bfloat16)
    tokens_v[...] = lax.dot_general(
        stack(table).astype(jnp.bfloat16),
        rows_v[:, :width],
        over_rows,
        preferred_element_type=jnp.float32,
    ).astype(jnp.bfloat16)
    copy = pltpu.make_async_copy(tokens_v, tokens_hbm, sems.at[0, 3])
    copy.start()
    copies.append(copy)
    slot_dw = sum(table[r] * tile(r, count - 1) for r in range(CAP))
    route = sum(chosen[s] * slot_dw[s : s + 1] for s in range(slots))
    route_ref[...] = (route / probs_ref[...].astype(jnp.float32)).astype(jnp.bfloat16)
    for copy in copies:
        copy.wait()


def gradients(placement, ids, probs, arrived, slots, tokens):
    xs, gs, du, sc, back = arrived
    width, units = xs.shape[1], sc.shape[1]
    bf16 = jnp.bfloat16
    shape = functools.partial(jax.ShapeDtypeStruct, dtype=bf16)
    vmem, hbm = pl.BlockSpec(memory_space=pltpu.VMEM), pl.BlockSpec(memory_space=pl.ANY)
    return pl.pallas_call(
        functools.partial(gradient_kernel, slots),
        out_shape=(
            shape((width, units)),
            shape((width, units)),
            shape((units, width)),
            shape((tokens, width)),
            shape(probs.shape),
        ),
        in_specs=[pl.BlockSpec(memory_space=pltpu.SMEM)] + [vmem] * 7,
        out_specs=(hbm, hbm, hbm, hbm, vmem),
        scratch_shapes=[
            pltpu.VMEM((width, units), bf16),
            pltpu.VMEM((width, units), bf16),
            pltpu.VMEM((units, width), bf16),
            pltpu.VMEM((tokens, width), bf16),
            pltpu.VMEM((32, width + LANES), bf16),
            pltpu.SemaphoreType.DMA((7, 4)),
        ],
        compiler_params=pltpu.CompilerParams(vmem_limit_bytes=36 * 2**20),
    )(placement, ids, probs, xs, gs, du, sc, back)


def on_small_slice(
    layer_input, output_grad, expert_ids, gate_probs, placement, gate_weight, up_weight, down_weight
):
    slots = lax.axis_size("expert")
    groups = lax.axis_size("dp")
    ids, probs = expert_ids.T, gate_probs.T
    arrived = exchange(
        ids,
        probs,
        placement,
        layer_input,
        output_grad,
        gate_weight[0],
        up_weight[0],
        down_weight[0],
        groups,
        slots,
    )
    grad_gate, grad_up, grad_down, grad_tokens, grad_route = gradients(
        placement, ids, probs, arrived, slots, layer_input.shape[0]
    )
    return grad_tokens, grad_route.T, grad_gate[None], grad_up[None], grad_down[None]


def solution(mesh):
    in_specs = (
        P(("dp", "expert"), None),
        P(("dp", "expert"), None),
        P(("dp", "expert"), None),
        P(("dp", "expert"), None),
        P(),
        P("expert", None, "dp"),
        P("expert", None, "dp"),
        P("expert", "dp", None),
    )
    out_specs = (
        P(("dp", "expert"), None),
        P(("dp", "expert"), None),
        P("expert", None, "dp"),
        P("expert", None, "dp"),
        P("expert", "dp", None),
    )
    small = mesh.shape["dp"] == 4 and mesh.shape["expert"] == 8
    return jax.shard_map(
        on_small_slice if small else on_device, mesh=mesh, in_specs=in_specs, out_specs=out_specs, check_vma=False
    )
```

```python
import functools
import math

import jax
import jax.numpy as jnp
from jax import lax
from jax.experimental import pallas as pl
from jax.experimental.pallas import tpu as pltpu
from jax.sharding import PartitionSpec as P

MESH = pl.DeviceIdType.MESH

CAP = 3
ROWS = 8
LANES = 128
CHUNKS = 4
TILE = 256
LINES = 2


def routes(expert_ids, gate_probs, placement):
    tokens = expert_ids.shape[0]
    slots = placement.shape[0]
    ids = expert_ids.T
    probs = gate_probs.T.astype(jnp.float32)
    topk = ids.shape[0]
    same = placement[:, None] == placement[None, :]
    slot = jnp.arange(slots, dtype=jnp.int32)
    copies = jnp.sum(same.astype(jnp.int32), axis=1)
    rank = jnp.sum((same & (slot[None, :] < slot[:, None])).astype(jnp.int32), axis=1)
    turn = jnp.arange(tokens, dtype=jnp.int32)[None, :] + jnp.arange(topk, dtype=jnp.int32)[:, None]
    chosen = (ids[None] == placement[:, None, None]) & (
        turn[None] % copies[:, None, None] == rank[:, None, None]
    )
    chosen = chosen.astype(jnp.float32)
    hit = jnp.sum(chosen, axis=1)
    weight = jnp.sum(chosen * probs[None], axis=1)
    token = jnp.arange(tokens, dtype=jnp.int32)
    before = (token[:, None] < token[None, :]).astype(jnp.bfloat16)
    position = jnp.dot(hit.astype(jnp.bfloat16), before, preferred_element_type=jnp.float32)
    place = jnp.arange(CAP, dtype=jnp.float32)
    table = hit[:, None, :] * (position[:, None, :] == place[None, :, None]).astype(jnp.float32)
    row_w = jnp.sum(table * weight[:, None, :], axis=-1)
    return chosen, table, row_w, same & (slot[:, None] != slot[None, :])


def meet(groups, slots):
    d, e = lax.axis_index("dp"), lax.axis_index("expert")
    barrier = pltpu.get_barrier_semaphore()
    for k in range(1, groups):
        pl.semaphore_signal(
            barrier, inc=1, device_id=(lax.rem(d + k, groups), e), device_id_type=MESH
        )
    for k in range(1, slots):
        pl.semaphore_signal(
            barrier, inc=1, device_id=(d, lax.rem(e + k, slots)), device_id_type=MESH
        )
    pl.semaphore_wait(barrier, groups + slots - 2)


def spread_kernel(
    groups, slots, u_ref, e_ref, out_ref, landed, ready, z_send, z_recv, p_send, p_recv, own_sem
):
    d, e = lax.axis_index("dp"), lax.axis_index("expert")
    height = u_ref.shape[0]
    third = e_ref.shape[0]
    tail = ready.shape[3] - LANES
    chunk = tail // third
    meet(groups, slots)

    def onward(plane, source, way):
        return pltpu.make_async_remote_copy(
            src_ref=source,
            dst_ref=landed.at[plane],
            send_sem=z_send.at[way, plane],
            recv_sem=z_recv.at[plane],
            device_id=(d + 1 - 2 * way, e),
            device_id_type=MESH,
        )

    def across(plane, j):
        peer = lax.rem(e + j, slots)
        return pltpu.make_async_remote_copy(
            src_ref=ready.at[plane, peer],
            dst_ref=out_ref.at[plane * slots + e],
            send_sem=p_send.at[plane, j - 1],
            recv_sem=p_recv.at[plane, j - 1],
            device_id=(d, peer),
            device_id_type=MESH,
        )

    def stay(plane):
        return pltpu.make_async_copy(
            ready.at[plane, e], out_ref.at[plane * slots + e], own_sem.at[plane]
        )

    def share(plane, read):
        last = read(pl.ds(tail, chunk))
        for c in range(third):
            lanes = pl.ds(c * chunk, chunk)
            rows = jnp.dot(
                e_ref[c, :, :height], read(lanes), preferred_element_type=jnp.float32
            ) + jnp.dot(e_ref[c, :, height:], last, preferred_element_type=jnp.float32)
            for s in range(slots):
                ready[plane, s, :, lanes] = rows[s * ROWS : (s + 1) * ROWS].astype(jnp.bfloat16)
        rows = jnp.dot(
            e_ref[0, :, :height],
            read(pl.ds(tail + chunk, LANES)),
            preferred_element_type=jnp.float32,
        )
        for s in range(slots):
            ready[plane, s, :, pl.ds(tail, LANES)] = rows[s * ROWS : (s + 1) * ROWS].astype(
                jnp.bfloat16
            )
        for j in range(1, slots):
            across(plane, j).start()
        stay(plane).start()

    @pl.when(d + 1 < groups)
    def _():
        onward(d, u_ref, 0).start()

    @pl.when(d > 0)
    def _():
        onward(d, u_ref, 1).start()

    share(d, lambda lanes: u_ref[:, lanes])
    for hop in range(1, groups):
        for way in range(2):
            plane = d - hop if way == 0 else d + hop
            more = d + 1 < groups if way == 0 else d > 0
            here = plane >= 0 if way == 0 else plane < groups

            @pl.when(here)
            def _(plane=plane, more=more, way=way):
                onward(plane, landed.at[plane], way).wait_recv()

                @pl.when(more)
                def _():
                    onward(plane, landed.at[plane], way).start()

                share(plane, lambda lanes: landed[plane, :, lanes])

    for plane in range(groups):

        @pl.when((plane <= d) & (d + 1 < groups))
        def _():
            onward(plane, landed.at[plane], 0).wait_send()

        @pl.when((plane >= d) & (d > 0))
        def _():
            onward(plane, landed.at[plane], 1).wait_send()

        for j in range(1, slots):
            across(plane, j).wait()
        stay(plane).wait()


def dispatch(unique, expand, groups, slots):
    height, width = unique.shape
    packed = 3 * (width - LANES) // 4 + LANES
    landed = (groups, height, width)
    ready = (groups, slots, ROWS, packed)
    need = 2 * (math.prod(landed) + math.prod(ready) + 2 * height * width)
    return pl.pallas_call(
        functools.partial(spread_kernel, groups, slots),
        out_shape=jax.ShapeDtypeStruct((groups * slots, ROWS, packed), jnp.bfloat16),
        in_specs=[pl.BlockSpec(memory_space=pltpu.VMEM)] * 2,
        out_specs=pl.BlockSpec(memory_space=pl.ANY),
        scratch_shapes=[
            pltpu.VMEM(landed, jnp.bfloat16),
            pltpu.VMEM(ready, jnp.bfloat16),
            pltpu.SemaphoreType.DMA((2, groups)),
            pltpu.SemaphoreType.DMA((groups,)),
            pltpu.SemaphoreType.DMA((groups, slots - 1)),
            pltpu.SemaphoreType.DMA((groups, slots - 1)),
            pltpu.SemaphoreType.DMA((groups,)),
        ],
        compiler_params=pltpu.CompilerParams(
            collective_id=0, has_side_effects=True, vmem_limit_bytes=need + 8 * 2**20
        ),
    )(unique, expand)


def arrival_order(groups):
    return sorted(range(1, groups), key=lambda k: (-min(k, groups - k), k))


def fold_kernel(
    groups, slots, p_ref, e_ref, out_ref, landed, sums, z_send, z_recv, p_send, p_recv, own_sem
):
    d, e = lax.axis_index("dp"), lax.axis_index("expert")
    width = p_ref.shape[2]
    step = (width // LANES // CHUNKS) * LANES
    cuts = [pl.ds(c * step, step if c < CHUNKS - 1 else width - c * step) for c in range(CHUNKS)]
    meet(groups, slots)
    along, moved = [], []
    for c, lanes in enumerate(cuts):
        for k in arrival_order(groups):
            plane = lax.rem(d + k, groups)
            copy = pltpu.make_async_remote_copy(
                src_ref=p_ref.at[plane, :, lanes],
                dst_ref=landed.at[k - 1, :, lanes],
                send_sem=z_send.at[c, k - 1],
                recv_sem=z_recv.at[c, k - 1],
                device_id=(plane, e),
                device_id_type=MESH,
            )
            copy.start()
            along.append((c, copy))
    for c, lanes in enumerate(cuts):
        for owner, copy in along:
            if owner == c:
                copy.wait_recv()
        total = p_ref[d, :, lanes].astype(jnp.float32)
        for k in range(1, groups):
            total = total + landed[k - 1, :, lanes].astype(jnp.float32)
        rows = jnp.dot(e_ref[...], total.astype(jnp.bfloat16), preferred_element_type=jnp.float32)
        for s in range(slots):
            sums[s, :, lanes] = rows[s * ROWS : (s + 1) * ROWS].astype(jnp.bfloat16)
        for j in range(1, slots):
            peer = lax.rem(e + j, slots)
            copy = pltpu.make_async_remote_copy(
                src_ref=sums.at[peer, :, lanes],
                dst_ref=out_ref.at[e, :, lanes],
                send_sem=p_send.at[c, j - 1],
                recv_sem=p_recv.at[c, j - 1],
                device_id=(d, peer),
                device_id_type=MESH,
            )
            copy.start()
            moved.append(copy)
    kept = pltpu.make_async_copy(sums.at[e], out_ref.at[e], own_sem)
    kept.start()
    for _, copy in along:
        copy.wait_send()
    for copy in moved:
        copy.wait()
    kept.wait()


def combine(partial, expand, groups, slots):
    _, height, width = partial.shape
    need = 2 * (2 * groups * height * width + slots * ROWS * width)
    return pl.pallas_call(
        functools.partial(fold_kernel, groups, slots),
        out_shape=jax.ShapeDtypeStruct((slots, ROWS, width), jnp.bfloat16),
        in_specs=[pl.BlockSpec(memory_space=pltpu.VMEM)] * 2,
        out_specs=pl.BlockSpec(memory_space=pl.ANY),
        scratch_shapes=[
            pltpu.VMEM((groups - 1, height, width), jnp.bfloat16),
            pltpu.VMEM((slots, ROWS, width), jnp.bfloat16),
            pltpu.SemaphoreType.DMA((CHUNKS, groups - 1)),
            pltpu.SemaphoreType.DMA((CHUNKS, groups - 1)),
            pltpu.SemaphoreType.DMA((CHUNKS, slots - 1)),
            pltpu.SemaphoreType.DMA((CHUNKS, slots - 1)),
            pltpu.SemaphoreType.DMA,
        ],
        compiler_params=pltpu.CompilerParams(
            collective_id=1, has_side_effects=True, vmem_limit_bytes=need + 8 * 2**20
        ),
    )(partial, expand)


def expert_kernel(
    a_ref, gate_ref, up_ref, down_ref, gg_ref, gu_ref, gd_ref, part_ref, g_ref, du_ref, sc_ref
):
    count = a_ref.shape[0]
    width, units = gate_ref.shape
    packed = a_ref.shape[1] - LANES
    rest = packed // CAP
    own_rows = TILE // ROWS * CAP
    over_units = (((1,), (1,)), ((), ()))
    over_rows = (((0,), (0,)), ((), ()))

    @pl.loop(0, count // TILE)
    def _(t):
        here = pl.ds(pl.multiple_of(t * TILE, TILE), TILE)
        row = lax.broadcasted_iota(jnp.int32, (TILE, TILE), 0)
        col = lax.broadcasted_iota(jnp.int32, (TILE, TILE), 1)
        place = row % ROWS
        source = row - place + 2 * CAP + (place >= CAP).astype(jnp.int32)
        tail = jnp.zeros((TILE, rest), jnp.float32)
        for c in range(CAP):
            pick = (col == source) & (place < 2 * CAP) & (place % CAP == c)
            tail = tail + jnp.dot(
                pick.astype(jnp.float32).astype(jnp.bfloat16),
                a_ref[here, c * rest : (c + 1) * rest],
                preferred_element_type=jnp.float32,
            )
        g_ref[here, : packed - width] = a_ref[here, width:packed]
        g_ref[here, packed - width :] = tail.astype(jnp.bfloat16)
        flat_x = a_ref[here, :width]
        scale = a_ref[here, packed : packed + LANES].astype(jnp.float32)[:, :1]
        pre_gate = jnp.dot(flat_x, gate_ref[...], preferred_element_type=jnp.float32)
        pre_up = jnp.dot(flat_x, up_ref[...], preferred_element_type=jnp.float32)
        back = lax.dot_general(
            g_ref[here, :], down_ref[...], over_units, preferred_element_type=jnp.float32
        )
        sigma = jax.nn.sigmoid(pre_gate)
        active = pre_gate * sigma
        hidden = active * pre_up
        d_hidden = scale * back
        unit_row = lax.broadcasted_iota(jnp.int32, (TILE, units), 0)
        real = unit_row % ROWS < 2 * CAP

        def masked(values):
            return jnp.where(real, values, 0.0)

        d_up = masked(d_hidden * active).astype(jnp.bfloat16)
        d_gate = masked(d_hidden * pre_up * sigma * (1.0 + pre_gate * (1.0 - sigma))).astype(
            jnp.bfloat16
        )
        du_ref[here, :units] = d_gate
        du_ref[here, units:] = d_up
        sc_ref[here, :] = masked(scale * hidden).astype(jnp.bfloat16)
        part_dw = jnp.sum(masked(hidden * back), axis=1, keepdims=True)
        part_dw = jnp.broadcast_to(part_dw, (TILE, LANES)).astype(jnp.bfloat16)
        target = lax.broadcasted_iota(jnp.int32, (own_rows, TILE), 0)
        origin = lax.broadcasted_iota(jnp.int32, (own_rows, TILE), 1)
        keep = (origin == target // CAP * ROWS + target % CAP).astype(jnp.float32)
        keep = keep.astype(jnp.bfloat16)

        def own(values):
            return jnp.dot(keep, values, preferred_element_type=jnp.float32).astype(jnp.bfloat16)

        own_gate, own_up = own(d_gate), own(d_up)
        out = pl.ds(pl.multiple_of(t * own_rows, 8), own_rows)
        part = lax.dot_general(
            own_gate, gate_ref[...], over_units, preferred_element_type=jnp.float32
        ) + lax.dot_general(own_up, up_ref[...], over_units, preferred_element_type=jnp.float32)
        part_ref[out, :width] = part.astype(jnp.bfloat16)
        part_ref[out, width:] = own(part_dw)

    step = width // 7

    @pl.loop(0, 7)
    def _(c):
        lanes = pl.ds(pl.multiple_of(c * step, LANES), step)
        both = lax.dot_general(
            a_ref[:, lanes], du_ref[...], over_rows, preferred_element_type=jnp.float32
        )
        gg_ref[lanes, :] = both[:, :units].astype(jnp.bfloat16)
        gu_ref[lanes, :] = both[:, units:].astype(jnp.bfloat16)
        down = lax.dot_general(
            sc_ref[...], g_ref[:, lanes], over_rows, preferred_element_type=jnp.float32
        )
        gd_ref[:, lanes] = down.astype(jnp.bfloat16)


def expert_step(arrived, gate_block, up_block, down_block):
    count, packed = arrived.shape
    width, units = gate_block.shape
    part = (count // ROWS * CAP, width + LANES)
    need = 2 * (
        count * (packed + width + 3 * units) + 6 * width * units + part[0] * part[1]
    )
    shape = functools.partial(jax.ShapeDtypeStruct, dtype=jnp.bfloat16)
    return pl.pallas_call(
        expert_kernel,
        out_shape=(
            shape((width, units)),
            shape((width, units)),
            shape((units, width)),
            shape(part),
        ),
        in_specs=[pl.BlockSpec(memory_space=pltpu.VMEM)] * 4,
        out_specs=tuple([pl.BlockSpec(memory_space=pltpu.VMEM)] * 4),
        scratch_shapes=[
            pltpu.VMEM((count, width), jnp.bfloat16),
            pltpu.VMEM((count, 2 * units), jnp.bfloat16),
            pltpu.VMEM((count, units), jnp.bfloat16),
        ],
        compiler_params=pltpu.CompilerParams(
            vmem_limit_bytes=min(need + 16 * 2**20, 63 * 2**20)
        ),
    )(arrived, gate_block, up_block, down_block)


def on_device(
    layer_input, output_grad, expert_ids, gate_probs, placement, gate_weight, up_weight, down_weight
):
    slots = lax.axis_size("expert")
    groups = lax.axis_size("dp")
    tokens, width = layer_input.shape
    blocks = slots * groups
    chosen, table, row_w, twin = routes(expert_ids, gate_probs, placement)
    token_table = table.reshape(slots * CAP, tokens).astype(jnp.bfloat16)
    send_x = jnp.dot(token_table, layer_input, preferred_element_type=jnp.float32)
    send_g = jnp.dot(token_table, output_grad, preferred_element_type=jnp.float32)
    unique = jnp.concatenate(
        [send_x, send_g, jnp.broadcast_to(row_w.reshape(slots * CAP, 1), (slots * CAP, LANES))],
        axis=1,
    ).astype(jnp.bfloat16)

    row = jnp.arange(ROWS, dtype=jnp.int32)
    cap = jnp.arange(CAP, dtype=jnp.int32)
    eye = jnp.eye(slots, dtype=jnp.float32)[:, None, :, None]
    others = twin.astype(jnp.float32)[:, None, :, None]

    def layout(pick_mine, pick_theirs):
        spread = eye * pick_mine[None, :, None, :] + others * pick_theirs[None, :, None, :]
        return spread.reshape(slots * ROWS, slots * CAP)

    mine = (row[:, None] == cap[None, :]).astype(jnp.float32)
    theirs = (row[:, None] == cap[None, :] + CAP).astype(jnp.float32)
    main = layout(mine, theirs)
    expand = jnp.stack(
        [
            jnp.concatenate(
                [
                    main,
                    layout(
                        ((row[:, None] == 2 * CAP) & (cap[None, :] == c)).astype(jnp.float32),
                        ((row[:, None] == 2 * CAP + 1) & (cap[None, :] == c)).astype(jnp.float32),
                    ),
                ],
                axis=1,
            )
            for c in range(CAP)
        ]
    ).astype(jnp.bfloat16)

    arrived = dispatch(unique, expand, groups, slots)
    grad_gate, grad_up, grad_down, partial = expert_step(
        arrived.reshape(blocks * ROWS, arrived.shape[2]),
        gate_weight[0],
        up_weight[0],
        down_weight[0],
    )
    partial = partial.reshape(groups, slots * CAP, width + LANES)
    spread = (eye * mine[None, :, None, :]).reshape(slots * ROWS, slots * CAP).astype(jnp.bfloat16)
    back_rows = combine(partial, spread, groups, slots).reshape(slots * ROWS, width + LANES)

    wide = jnp.einsum("rc,sct->srt", mine, table).reshape(slots * ROWS, tokens).astype(jnp.bfloat16)
    grad_tokens = lax.dot_general(
        wide, back_rows[:, :width], (((0,), (0,)), ((), ())), preferred_element_type=jnp.float32
    ).astype(jnp.bfloat16)
    row_dw = back_rows[:, width].astype(jnp.float32)
    slot_dw = jnp.sum(
        (wide.astype(jnp.float32) * row_dw[:, None]).reshape(slots, ROWS, tokens), axis=1
    )
    grad_route = jnp.sum(chosen * slot_dw[:, None, :], axis=0).T.astype(jnp.bfloat16)
    return (
        grad_tokens,
        grad_route,
        grad_gate[None],
        grad_up[None],
        grad_down[None],
    )


def swap(count):
    row = lax.broadcasted_iota(jnp.int32, (count, count), 0)
    col = lax.broadcasted_iota(jnp.int32, (count, count), 1)
    return (col == row % 8 * 8 + row // 8).astype(jnp.float32).astype(jnp.bfloat16)


def one_hot_dot(table, values):
    return jnp.dot(table, values, preferred_element_type=jnp.float32)


def pick(place_ref, ids, slots):
    held = [place_ref[s] for s in range(slots)]
    turn = lax.broadcasted_iota(jnp.int32, ids.shape, 0) + lax.broadcasted_iota(
        jnp.int32, ids.shape, 1
    )
    chosen = []
    for s in range(slots):
        same = [(held[s] == held[q]).astype(jnp.int32) for q in range(slots)]
        copies, rank = sum(same), sum(same[:s], jnp.int32(0))
        chosen.append(
            ((ids == held[s]) & ((turn & (copies - 1)) == rank)).astype(jnp.float32)
        )
    return chosen


def tables(chosen):
    hit = jnp.concatenate([jnp.sum(c, axis=0, keepdims=True) for c in chosen], axis=0)
    tokens = hit.shape[1]
    row = lax.broadcasted_iota(jnp.int32, (tokens, tokens), 0)
    col = lax.broadcasted_iota(jnp.int32, (tokens, tokens), 1)
    before = (row < col).astype(jnp.float32).astype(jnp.bfloat16)
    position = one_hot_dot(hit.astype(jnp.bfloat16), before)
    return [jnp.where(position == float(r), hit, 0.0) for r in range(CAP)]


def stack(parts):
    return jnp.concatenate([*parts, jnp.zeros_like(parts[0])], axis=0)


def twin_of(place_ref, slots, e):
    mine = jnp.int32(0)
    for s in range(slots):
        mine = jnp.where(e == s, place_ref[s], mine)
    found, other = jnp.int32(0), jnp.int32(0)
    for s in range(slots):
        same = ((place_ref[s] == mine) & (e != s)).astype(jnp.int32)
        found = found + same
        other = other + same * s
    return found > 0, other


def exchange_kernel(
    groups,
    slots,
    place_hbm,
    ids_hbm,
    probs_hbm,
    x_hbm,
    g_hbm,
    gate_hbm,
    up_hbm,
    down_hbm,
    xs_ref,
    gs_ref,
    du_ref,
    sc_ref,
    back_ref,
    place_ref,
    ids_ref,
    probs_ref,
    x_v,
    g_v,
    gate_v,
    up_v,
    down_v,
    packed,
    landed,
    partner,
    export,
    xin,
    onward,
    yin,
    twins,
    parts,
    agg,
    total,
    ret,
    load_sem,
    a_send,
    a_recv,
    z_send,
    z_recv,
    c_send,
    c_recv,
    x_send,
    x_recv,
    y_send,
    y_recv,
    t_send,
    t_recv,
    f_send,
    f_recv,
    r_send,
    r_recv,
    own_sem,
):
    d, e = lax.axis_index("dp"), lax.axis_index("expert")
    core, ex, ey = e % 2, e // 2 % 2, e // 4
    to_core, to_x, to_y = e + 1 - 2 * core, e + 2 - 4 * ex, e + 4 - 8 * ey
    last = groups - 1
    width = x_v.shape[1]
    piece = 2 * width // 8
    units = gate_v.shape[1]
    count = parts.shape[1]
    over_units = (((1,), (1,)), ((), ()))
    half = pl.ds(core * 4, 4)
    rest = pl.ds(4 - core * 4, 4)

    get_x = pltpu.make_async_copy(x_hbm, x_v, load_sem.at[0])
    get_g = pltpu.make_async_copy(g_hbm, g_v, load_sem.at[1])
    get_w = [
        pltpu.make_async_copy(gate_hbm, gate_v, load_sem.at[2]),
        pltpu.make_async_copy(up_hbm, up_v, load_sem.at[3]),
        pltpu.make_async_copy(down_hbm, down_v, load_sem.at[4]),
    ]
    get_routes = [
        pltpu.make_async_copy(place_hbm, place_ref, load_sem.at[5]),
        pltpu.make_async_copy(ids_hbm, ids_ref, load_sem.at[6]),
        pltpu.make_async_copy(probs_hbm, probs_ref, load_sem.at[7]),
    ]
    for copy in (*get_routes, get_x, get_g):
        copy.start()
    barrier = pltpu.get_barrier_semaphore()

    @pl.when(d < last)
    def _():
        pl.semaphore_signal(barrier, inc=1, device_id=(d + 1, e), device_id_type=MESH)

    @pl.when(d > 0)
    def _():
        pl.semaphore_signal(barrier, inc=1, device_id=(d - 1, e), device_id_type=MESH)

    for k in range(1, slots):
        pl.semaphore_signal(
            barrier, inc=1, device_id=(d, lax.rem(e + k, slots)), device_id_type=MESH
        )
    for copy in get_routes:
        copy.wait()
    chosen = pick(place_ref, ids_ref[...], slots)
    table = tables(chosen)
    probs = probs_ref[...].astype(jnp.float32)
    weight = jnp.concatenate(
        [jnp.sum(c * probs, axis=0, keepdims=True) for c in chosen], axis=0
    )
    plain = stack(table).astype(jnp.bfloat16)
    scaled = stack([t * weight for t in table]).astype(jnp.bfloat16)
    turned = swap(8 * slots)
    get_x.wait()
    get_g.wait()
    for copy in get_w:
        copy.start()
    whole = [
        one_hot_dot(plain if j < 4 else scaled, source[:, j % 4 * piece : (j % 4 + 1) * piece])
        for j, source in enumerate([x_v] * 4 + [g_v] * 4)
    ]
    for r in range(CAP):
        gathered = jnp.concatenate([rows[r * 8 : (r + 1) * 8] for rows in whole], axis=0)
        moved = one_hot_dot(turned, gathered.astype(jnp.bfloat16))
        for s in range(slots):
            packed[s, :, r * piece : (r + 1) * piece] = moved[s * 8 : (s + 1) * 8].astype(
                jnp.bfloat16
            )
    pl.semaphore_wait(barrier, slots - 1 + (d > 0).astype(jnp.int32) + (d < last).astype(jnp.int32))

    def across(j):
        peer = lax.rem(e + j, slots)
        return pltpu.make_async_remote_copy(
            src_ref=packed.at[peer],
            dst_ref=landed.at[d, e],
            send_sem=a_send.at[j - 1],
            recv_sem=a_recv.at[e],
            device_id=(d, peer),
            device_id_type=MESH,
        )

    def arrival(b):
        return pltpu.make_async_remote_copy(
            src_ref=packed.at[b],
            dst_ref=landed.at[d, b],
            send_sem=a_send.at[0],
            recv_sem=a_recv.at[b],
            device_id=(d, b),
            device_id_type=MESH,
        )

    def along(plane, q, way):
        part = landed.at[plane, pl.ds(2 * q, 2)]
        return pltpu.make_async_remote_copy(
            src_ref=part,
            dst_ref=part,
            send_sem=z_send.at[way, plane, q],
            recv_sem=z_recv.at[plane, q],
            device_id=(d + 1 - 2 * way, e),
            device_id_type=MESH,
        )

    for j in range(1, slots):
        across(j).start()
    landed[d, e] = packed[e]
    middle = (d > 0).astype(jnp.int32) * (d < last).astype(jnp.int32)
    inward = d // 2
    outward = 1 - inward
    sign = 1 - 2 * inward
    order = [(ey + i // 2) % 2 * 2 + (ex + i % 2) % 2 for i in range(4)]
    for i, q in enumerate(order):
        for b in (2 * q, 2 * q + 1):

            @pl.when(b != e)
            def _(b=b):
                arrival(b).wait_recv()

        @pl.when((middle == 0) | (i < 2))
        def _(q=q):
            along(d, q, inward).start()

        @pl.when((middle == 1) & (i < 2))
        def _(q=q):
            along(d, q, outward).start()

    has, other = twin_of(place_ref, slots, e)
    core_has, core_other = twin_of(place_ref, slots, to_core)
    mine_out = has & (other // 2 != e // 2)
    core_out = core_has & (core_other // 2 != e // 2)
    target = jnp.where(mine_out, other, core_other) // 2
    from_x = target == to_x // 2

    def choose(first, a, b):
        keep = jnp.full(a.shape, first.astype(jnp.int32)) == 1
        return jnp.where(keep, a.astype(jnp.float32), b.astype(jnp.float32)).astype(jnp.bfloat16)

    def link(source, target_ref, sems, plane, device):
        return pltpu.make_async_remote_copy(
            src_ref=source,
            dst_ref=target_ref,
            send_sem=sems[0].at[plane],
            recv_sem=sems[1].at[plane],
            device_id=(d, device),
            device_id_type=MESH,
        )

    def core_copy(plane):
        return link(landed.at[plane], partner.at[plane], (c_send, c_recv), plane, to_core)

    def x_copy(plane):
        return link(export.at[plane], xin.at[plane], (x_send, x_recv), plane, to_x)

    def y_copy(plane):
        return link(onward.at[plane], yin.at[plane], (y_send, y_recv), plane, to_y)

    def half_copy(plane):
        part = twins.at[plane, half]
        return link(part, part, (t_send, t_recv), plane, to_core)

    def half_arrival(plane):
        part = twins.at[plane, rest]
        return link(part, part, (t_send, t_recv), plane, to_core)

    def relay_x(plane):
        core_copy(plane).wait_recv()
        for b in range(4):
            export[plane, b] = choose(
                mine_out, landed[plane, core * 4 + b], partner[plane, core * 4 + b]
            )
        x_copy(plane).start()

    def relay_y(plane):
        x_copy(plane).wait_recv()
        for b in range(4):
            onward[plane, b] = choose(mine_out | core_out, export[plane, b], xin[plane, b])
        y_copy(plane).start()

    def relay_half(plane):
        y_copy(plane).wait_recv()
        for b in range(4):
            twins[plane, core * 4 + b] = choose(from_x, xin[plane, b], yin[plane, b])
        half_copy(plane).start()

    def unpack(base, block):
        stacked = jnp.concatenate(
            [block(b).astype(jnp.float32) for b in range(8)], axis=0
        ).astype(jnp.bfloat16)
        moved = [
            one_hot_dot(turned, stacked[:, r * piece : (r + 1) * piece]) for r in range(CAP)
        ]
        for j in range(8):
            rows = stack([m[j * 8 : (j + 1) * 8] for m in moved]).astype(jnp.bfloat16)
            if j < 4:
                xs_ref[pl.ds(base, 32), j * piece : (j + 1) * piece] = rows
            else:
                gs_ref[pl.ds(base, 32), (j - 4) * piece : (j - 3) * piece] = rows

    def hidden_grads(base, count):
        rows_x = xs_ref[pl.ds(base, count), :]
        rows_g = gs_ref[pl.ds(base, count), :]
        pre_gate = jnp.dot(rows_x, gate_v[...], preferred_element_type=jnp.float32)
        pre_up = jnp.dot(rows_x, up_v[...], preferred_element_type=jnp.float32)
        back = lax.dot_general(
            rows_g, down_v[...], over_units, preferred_element_type=jnp.float32
        )
        sigma = jax.nn.sigmoid(pre_gate)
        active = pre_gate * sigma
        hidden = active * pre_up
        d_up = (back * active).astype(jnp.bfloat16)
        d_gate = (back * pre_up * sigma * (1.0 + pre_gate * (1.0 - sigma))).astype(jnp.bfloat16)
        du_ref[pl.ds(base, count), :units] = d_gate
        du_ref[pl.ds(base, count), units:] = d_up
        sc_ref[pl.ds(base, count), :] = hidden.astype(jnp.bfloat16)
        return d_gate, d_up, jnp.sum(hidden * back, axis=1, keepdims=True)

    def own_rows(plane):
        base = pl.multiple_of(plane * 32, 32)
        unpack(base, lambda b: landed[plane, b])
        d_gate, d_up, part_dw = hidden_grads(base, 32)
        part = lax.dot_general(
            d_gate, gate_v[...], over_units, preferred_element_type=jnp.float32
        ) + lax.dot_general(d_up, up_v[...], over_units, preferred_element_type=jnp.float32)
        part_dw = jnp.broadcast_to(part_dw, (32, LANES))
        for c in range(count):
            column = part[:, c * LANES : (c + 1) * LANES] if c < count - 1 else part_dw
            for r in range(CAP):
                parts[plane, c, r] = column[r * 8 : (r + 1) * 8].astype(jnp.bfloat16)

    def twin_rows(plane):
        base = pl.multiple_of(groups * 32 + plane * 32, 32)

        def block(b):
            near = partner[plane, b].astype(jnp.float32)
            far = twins[plane, b].astype(jnp.float32)
            take_far = jnp.full(near.shape, mine_out.astype(jnp.int32)) == 1
            take_any = jnp.full(near.shape, has.astype(jnp.int32)) == 1
            return jnp.where(take_any, jnp.where(take_far, far, near), 0.0)

        unpack(base, block)

    cuts = [count * l // LINES for l in range(LINES + 1)]
    cuts = [pl.ds(a, b - a) for a, b in zip(cuts[:-1], cuts[1:])]

    def home(way, plane, l):
        return pltpu.make_async_remote_copy(
            src_ref=parts.at[plane, cuts[l]],
            dst_ref=agg.at[way, plane, cuts[l]],
            send_sem=f_send.at[plane, l],
            recv_sem=f_recv.at[way, plane, l],
            device_id=(d + 1 - 2 * way, e),
            device_id_type=MESH,
        )

    def pass_on(way, plane, l):
        home(way, plane, l).wait_recv()
        both = parts[plane, cuts[l]].astype(jnp.float32) + agg[way, plane, cuts[l]].astype(
            jnp.float32
        )
        parts[plane, cuts[l]] = both.astype(jnp.bfloat16)
        home(way, plane, l).start()

    def finish():
        total[...] = parts[d].astype(jnp.float32)
        for way in range(2):

            @pl.when(d > 0 if way == 0 else d < last)
            def _(way=way):
                for l in range(LINES):
                    home(way, d, l).wait_recv()
                total[...] = total[...] + agg[way, d].astype(jnp.float32)

        columns = []
        for k in range(ret.shape[2] // LANES):
            tall = []
            for j in range(8):
                r, c = divmod(8 * k + j, count)
                tall.append(
                    total[c, r]
                    if r < CAP
                    else jnp.zeros((8, LANES), jnp.float32)
                )
            columns.append(jnp.concatenate(tall, axis=0))
        moved = one_hot_dot(turned, jnp.concatenate(columns, axis=1).astype(jnp.bfloat16))
        for s in range(slots):
            ret[s] = moved[s * 8 : (s + 1) * 8].astype(jnp.bfloat16)
        for j in range(1, slots):
            back_copy(j).start()
        kept().start()

    def back_copy(j):
        peer = lax.rem(e + j, slots)
        return pltpu.make_async_remote_copy(
            src_ref=ret.at[peer],
            dst_ref=back_ref.at[e],
            send_sem=r_send.at[j - 1],
            recv_sem=r_recv.at[j - 1],
            device_id=(d, peer),
            device_id_type=MESH,
        )

    def kept():
        return pltpu.make_async_copy(ret.at[e], back_ref.at[e], own_sem)

    beside, far, near = d - sign, d + 2 * sign, d + sign

    def nth(n):
        return d + sign * ((4 - n) % 4 - 4 * middle * ((n + 3) // 4 - (n + 2) // 4))

    def forward(plane, q, way):
        along(plane, q, way).wait_recv()
        along(plane, q, way).start()

    def middle_first():
        for i in range(4):
            forward(beside, order[i], inward)
            forward(near if i < 2 else far, order[i % 2], outward)
        for q in order[2:]:
            along(d, q, inward).start()
        along(d, order[2], outward).start()

    def middle_second():
        for q in order[2:]:
            forward(far, q, outward)
        along(d, order[3], outward).start()

    def middle_third():
        for q in order[2:]:
            forward(near, q, outward)

    for copy in get_w:
        copy.wait()

    @pl.loop(0, groups + 3)
    def _(n):
        for step, arrive in enumerate((middle_first, middle_second, middle_third)):

            @pl.when((middle == 1) & (n == step + 1))
            def _(arrive=arrive):
                arrive()

        @pl.when(n < groups)
        def _():
            plane = nth(n)

            @pl.when((middle == 0) & (n > 0))
            def _():
                for q in order:
                    along(plane, q, inward).wait_recv()

            core_copy(plane).start()
            own_rows(plane)

            @pl.when((middle == 0) & (n > 0))
            def _():
                for l in range(LINES):
                    home(inward, plane, l).start()

            relay_x(plane)

        @pl.when((n > 0) & (n <= groups))
        def _():
            relay_y(nth(n - 1))

        @pl.when((n == groups) & (middle == 1))
        def _():
            for l in range(LINES):
                pass_on(inward, far, l)
            for l in range(LINES):
                pass_on(outward, beside, l)

        @pl.when(n == groups + 1)
        def _():
            @pl.when(middle == 1)
            def _():
                for l in range(LINES):
                    pass_on(inward, near, l)

            finish()

        @pl.when((n > 1) & (n <= groups + 1))
        def _():
            relay_half(nth(n - 2))

        @pl.when(n > 2)
        def _():
            plane = nth(n - 3)
            half_arrival(plane).wait_recv()
            twin_rows(plane)

    hidden_grads(groups * 32, groups * 32)

    for j in range(1, slots):
        across(j).wait_send()
        back_copy(j).wait()
    kept().wait()
    for plane in range(groups):
        for q in range(4):

            @pl.when((plane <= d) & (d < last))
            def _(plane=plane, q=q):
                along(plane, q, 0).wait_send()

            @pl.when((plane >= d) & (d > 0))
            def _(plane=plane, q=q):
                along(plane, q, 1).wait_send()

        core_copy(plane).wait_send()
        x_copy(plane).wait_send()
        y_copy(plane).wait_send()
        half_copy(plane).wait_send()
        for l in range(LINES):
            for way in range(2):

                @pl.when(plane > d if way == 0 else plane < d)
                def _(plane=plane, way=way, l=l):
                    home(way, plane, l).wait_send()


def exchange(ids, probs, placement, x, g, gate, up, down, groups, slots):
    tokens, width = x.shape
    units = gate.shape[1]
    piece = width // 4
    full = width + LANES
    back = pl.cdiv(CAP * full, 8 * LANES) * LANES
    rows = 2 * groups * 32
    bf16 = jnp.bfloat16
    shape = functools.partial(jax.ShapeDtypeStruct, dtype=bf16)
    vmem, hbm = pl.BlockSpec(memory_space=pltpu.VMEM), pl.BlockSpec(memory_space=pltpu.HBM)
    dma = pltpu.SemaphoreType.DMA
    planes = (groups, 8, 8, CAP * piece)
    halves = (groups, 4, 8, CAP * piece)
    return pl.pallas_call(
        functools.partial(exchange_kernel, groups, slots),
        out_shape=(
            shape((rows, width)),
            shape((rows, width)),
            shape((rows, 2 * units)),
            shape((rows, units)),
            shape((slots, 8, back)),
        ),
        in_specs=[hbm] * 8,
        out_specs=(vmem, vmem, vmem, vmem, pl.BlockSpec(memory_space=pl.ANY)),
        scratch_shapes=[
            pltpu.SMEM(placement.shape, jnp.int32),
            pltpu.VMEM(ids.shape, jnp.int32),
            pltpu.VMEM(probs.shape, bf16),
            pltpu.VMEM((tokens, width), bf16),
            pltpu.VMEM((tokens, width), bf16),
            pltpu.VMEM((width, units), bf16),
            pltpu.VMEM((width, units), bf16),
            pltpu.VMEM((units, width), bf16),
            pltpu.VMEM((slots, 8, CAP * piece), bf16),
            pltpu.VMEM(planes, bf16),
            pltpu.VMEM(planes, bf16),
            pltpu.VMEM(halves, bf16),
            pltpu.VMEM(halves, bf16),
            pltpu.VMEM(halves, bf16),
            pltpu.VMEM(halves, bf16),
            pltpu.VMEM(planes, bf16),
            pltpu.VMEM((groups, full // LANES, CAP, 8, LANES), bf16),
            pltpu.VMEM((2, groups, full // LANES, CAP, 8, LANES), bf16),
            pltpu.VMEM((full // LANES, CAP, 8, LANES), jnp.float32),
            pltpu.VMEM((slots, 8, back), bf16),
            dma((8,)),
            dma((slots - 1,)),
            dma((slots,)),
            dma((2, groups, 4)),
            dma((groups, 4)),
            dma((groups,)),
            dma((groups,)),
            dma((groups,)),
            dma((groups,)),
            dma((groups,)),
            dma((groups,)),
            dma((groups,)),
            dma((groups,)),
            dma((groups, LINES)),
            dma((2, groups, LINES)),
            dma((slots - 1,)),
            dma((slots - 1,)),
            dma,
        ],
        compiler_params=pltpu.CompilerParams(
            collective_id=2, has_side_effects=True, vmem_limit_bytes=36 * 2**20
        ),
    )(
        *(
            pltpu.with_memory_space_constraint(value, pltpu.HBM)
            for value in (placement, ids, probs, x, g, gate, up, down)
        )
    )


def gradient_kernel(
    slots,
    place_ref,
    ids_ref,
    probs_ref,
    xs_ref,
    gs_ref,
    du_ref,
    sc_ref,
    back_ref,
    gg_hbm,
    gu_hbm,
    gd_hbm,
    tokens_hbm,
    route_ref,
    gg_v,
    gu_v,
    gd_v,
    tokens_v,
    rows_v,
    sems,
):
    width = xs_ref.shape[1]
    units = sc_ref.shape[1]
    steps = 7
    step = width // steps
    over_rows = (((0,), (0,)), ((), ()))
    copies = []
    for c in range(steps):
        lanes = pl.ds(c * step, step)
        both = lax.dot_general(
            xs_ref[:, lanes], du_ref[...], over_rows, preferred_element_type=jnp.float32
        )
        gg_v[lanes, :] = both[:, :units].astype(jnp.bfloat16)
        gu_v[lanes, :] = both[:, units:].astype(jnp.bfloat16)
        gd_v[:, lanes] = lax.dot_general(
            sc_ref[...], gs_ref[:, lanes], over_rows, preferred_element_type=jnp.float32
        ).astype(jnp.bfloat16)
        for i, (source, target) in enumerate(
            [
                (gg_v.at[lanes, :], gg_hbm.at[lanes, :]),
                (gu_v.at[lanes, :], gu_hbm.at[lanes, :]),
                (gd_v.at[:, lanes], gd_hbm.at[:, lanes]),
            ]
        ):
            copy = pltpu.make_async_copy(source, target, sems.at[c, i])
            copy.start()
            copies.append(copy)

    chosen = pick(place_ref, ids_ref[...], slots)
    table = tables(chosen)
    stacked = jnp.concatenate(
        [back_ref[s].astype(jnp.float32) for s in range(slots)], axis=0
    ).astype(jnp.bfloat16)
    moved = one_hot_dot(swap(8 * slots), stacked)
    count = rows_v.shape[1] // LANES

    def tile(r, c):
        k, j = divmod(r * count + c, 8)
        return moved[j * 8 : (j + 1) * 8, k * LANES : (k + 1) * LANES]

    for c in range(count - 1):
        rows_v[:, c * LANES : (c + 1) * LANES] = stack(
            [tile(r, c) for r in range(CAP)]
        ).astype(jnp.bfloat16)
    tokens_v[...] = lax.dot_general(
        stack(table).astype(jnp.bfloat16),
        rows_v[:, :width],
        over_rows,
        preferred_element_type=jnp.float32,
    ).astype(jnp.bfloat16)
    copy = pltpu.make_async_copy(tokens_v, tokens_hbm, sems.at[0, 3])
    copy.start()
    copies.append(copy)
    slot_dw = sum(table[r] * tile(r, count - 1) for r in range(CAP))
    route = sum(chosen[s] * slot_dw[s : s + 1] for s in range(slots))
    route_ref[...] = (route / probs_ref[...].astype(jnp.float32)).astype(jnp.bfloat16)
    for copy in copies:
        copy.wait()


def gradients(placement, ids, probs, arrived, slots, tokens):
    xs, gs, du, sc, back = arrived
    width, units = xs.shape[1], sc.shape[1]
    bf16 = jnp.bfloat16
    shape = functools.partial(jax.ShapeDtypeStruct, dtype=bf16)
    vmem, hbm = pl.BlockSpec(memory_space=pltpu.VMEM), pl.BlockSpec(memory_space=pl.ANY)
    return pl.pallas_call(
        functools.partial(gradient_kernel, slots),
        out_shape=(
            shape((width, units)),
            shape((width, units)),
            shape((units, width)),
            shape((tokens, width)),
            shape(probs.shape),
        ),
        in_specs=[pl.BlockSpec(memory_space=pltpu.SMEM)] + [vmem] * 7,
        out_specs=(hbm, hbm, hbm, hbm, vmem),
        scratch_shapes=[
            pltpu.VMEM((width, units), bf16),
            pltpu.VMEM((width, units), bf16),
            pltpu.VMEM((units, width), bf16),
            pltpu.VMEM((tokens, width), bf16),
            pltpu.VMEM((32, width + LANES), bf16),
            pltpu.SemaphoreType.DMA((7, 4)),
        ],
        compiler_params=pltpu.CompilerParams(vmem_limit_bytes=36 * 2**20),
    )(placement, ids, probs, xs, gs, du, sc, back)


def on_small_slice(
    layer_input, output_grad, expert_ids, gate_probs, placement, gate_weight, up_weight, down_weight
):
    slots = lax.axis_size("expert")
    groups = lax.axis_size("dp")
    ids, probs = expert_ids.T, gate_probs.T
    arrived = exchange(
        ids,
        probs,
        placement,
        layer_input,
        output_grad,
        gate_weight[0],
        up_weight[0],
        down_weight[0],
        groups,
        slots,
    )
    grad_gate, grad_up, grad_down, grad_tokens, grad_route = gradients(
        placement, ids, probs, arrived, slots, layer_input.shape[0]
    )
    return grad_tokens, grad_route.T, grad_gate[None], grad_up[None], grad_down[None]


def solution(mesh):
    in_specs = (
        P(("dp", "expert"), None),
        P(("dp", "expert"), None),
        P(("dp", "expert"), None),
        P(("dp", "expert"), None),
        P(),
        P("expert", None, "dp"),
        P("expert", None, "dp"),
        P("expert", "dp", None),
    )
    out_specs = (
        P(("dp", "expert"), None),
        P(("dp", "expert"), None),
        P("expert", None, "dp"),
        P("expert", None, "dp"),
        P("expert", "dp", None),
    )
    small = mesh.shape["dp"] == 4 and mesh.shape["expert"] == 8
    return jax.shard_map(
        on_small_slice if small else on_device, mesh=mesh, in_specs=in_specs, out_specs=out_specs, check_vma=False
    )
```
